256 devices in a mesh: rx: 32 (over z, y_hi, core), tm: 8 (over y_lo, x).
Axes of the slice: x: 4, y: 4 (y_hi: 2, y_lo: 2; y = y_hi * 2 + y_lo), z: 8, core: 2. Of those that a mesh axis runs over, the one named last changes fastest.
Arguments:
- signals: float32 [2, 32, 524288], P(None, 'rx', 'tm'), may hold values from -6 to 6
Outputs:
- ambiguity: float32 [256, 2, 32, 4, 1, 256], P('tm', None, 'rx')
The draws below stay inside these ranges and needn't reach their ends.
All inputs are finite; a program needn't handle non-finite values.
Results may differ from the reference program's by a relative error of at most 0.0003.
Values sent between devices are 32-bit elements; how exact they have to be, the bound alone decides.
A program may use at most 64 MiB of HBM per device.

```python
import math
import jax
import jax.numpy as jnp
from jax import lax

SEG_LEN = 4096
LAGS = 256
DOPLEN = 512
DOPK = 256
OFFS = 4
REC_DEV = 1
REC = 32
SEGS = 128
SAMPLES = 524288
N_RX = 32


def level_of(rng, extent, pieces, smallest, top_value):
    loudness, own = 1.0, jax.random.fold_in(rng, 6)
    for position, parts in pieces:
        steps = jnp.exp(jax.random.uniform(jax.random.fold_in(own, position), (parts,), jnp.float32, smallest / len(pieces), top_value / len(pieces)))
        loudness = loudness * jnp.repeat(steps, extent[position] // parts).reshape([-1 if axis == position else 1 for axis in range(len(extent))])
    return loudness


def gaussian(own_key, extent, deviation, limit, pieces=(), kind=jnp.bfloat16):
    values = jax.random.normal(own_key, extent, jnp.float32) * deviation
    if len(pieces) > 0:
        values = level_of(own_key, extent, pieces, -0.22, 0.18) * values
    return jnp.clip(values, min=-limit, max=limit).astype(kind)


def setup_inputs(seed: int = 0) -> dict:
    arg_keys = jax.random.split(jax.random.key(seed), 2)
    return {
        "signals": gaussian(arg_keys[0], (2, REC, SAMPLES), 1.0, 6.0, ((1, 32), (2, 8)), jnp.float32),
    }


def reference(signals):
    field = lax.complex(signals[0], signals[1])
    segments = field.reshape(REC, SEGS, SEG_LEN)
    spectra = jnp.fft.fft(segments, axis=-1)
    half = LAGS // 2
    seg_index = jnp.arange(SEGS, dtype=jnp.int32)
    freq_index = jnp.arange(DOPK, dtype=jnp.int32) - DOPK // 2
    phase = (seg_index[:, None] * freq_index[None, :] % DOPLEN).astype(jnp.float32)
    angle = 2.0 * math.pi / DOPLEN * phase
    dop_cos = jnp.cos(angle)
    dop_sin = -jnp.sin(angle)
    highest = lax.Precision.HIGHEST

    def one_group(group):
        own = lax.dynamic_slice_in_dim(spectra, (group * REC_DEV).astype(jnp.int32), REC_DEV, 0)
        blocks = []
        for step in range(1, OFFS + 1):
            far_group = ((group - step) % N_RX).astype(jnp.int32)
            far = lax.dynamic_slice_in_dim(spectra, far_group * REC_DEV, REC_DEV, 0)
            product = own[:, None] * jnp.conj(far[None])
            full = jnp.fft.ifft(product, axis=-1)
            kept = jnp.concatenate([full[..., SEG_LEN - half:], full[..., :half]], axis=-1)
            corr_re = jnp.real(kept)
            corr_im = jnp.imag(kept)
            amb_re = jnp.einsum('absl,sf->labf', corr_re, dop_cos, precision=highest) - jnp.einsum('absl,sf->labf', corr_im, dop_sin, precision=highest)
            amb_im = jnp.einsum('absl,sf->labf', corr_re, dop_sin, precision=highest) + jnp.einsum('absl,sf->labf', corr_im, dop_cos, precision=highest)
            blocks.append(jnp.stack([amb_re, amb_im], axis=1))
        return jnp.stack(blocks, axis=3)
    groups = lax.map(one_group, jnp.arange(N_RX, dtype=jnp.int32))
    scale = 1.0 / math.sqrt(2.0 * SEG_LEN * SEGS)
    result = jnp.moveaxis(groups, 0, 2).reshape(LAGS, 2, REC, OFFS, REC_DEV, DOPK) * scale
    return result.astype(jnp.float32)
```

```python
import math

import jax
import jax.numpy as jnp
import numpy as np
from jax import lax
from jax.sharding import PartitionSpec as P

SEG_LEN = 4096
LAGS = 256
DOPLEN = 512
DOPK = 256
OFFS = 4
BLOCK = 256
WINDOW = 512

PRECISION = lax.Precision.HIGH


def forward_table():
    sample = np.arange(WINDOW)[:, None]
    freq = np.arange(WINDOW // 2)[None, :] + 0.5
    angle = 2.0 * np.pi / WINDOW * sample * freq
    return np.concatenate([np.cos(angle), np.sin(angle)], axis=1).astype(np.float32)


def inverse_table():
    lag = np.arange(LAGS)[None, :]
    freq = np.arange(WINDOW // 2)[:, None] + 0.5
    angle = 2.0 * np.pi / WINDOW * lag * freq
    return (np.concatenate([np.cos(angle), np.sin(angle)], axis=0) / WINDOW).astype(np.float32)


def doppler_table(segs):
    seg = np.arange(segs)[:, None]
    freq = np.arange(DOPK)[None, :] - DOPK // 2
    angle = 2.0 * np.pi / DOPLEN * (seg * freq % DOPLEN)
    scale = 1.0 / math.sqrt(2.0 * SEG_LEN * segs)
    cos, sin = np.cos(angle) * scale, -np.sin(angle) * scale
    return np.concatenate(
        [np.concatenate([cos, sin], axis=1), np.concatenate([-sin, cos], axis=1)], axis=0
    ).astype(np.float32)


def shifted(value, axis, steps):
    count = lax.axis_size(axis)
    pairs = [(source, (source + steps) % count) for source in range(count)]
    return lax.ppermute(value, axis, pairs)


def spectra(rows, table):
    half = WINDOW // 2
    mixed = jnp.dot(rows, table, precision=PRECISION)
    a_cos, a_sin = mixed[0, ..., :half], mixed[0, ..., half:]
    b_cos, b_sin = mixed[1, ..., :half], mixed[1, ..., half:]
    return a_cos + b_sin, b_cos - a_sin, a_cos - b_sin, b_cos + a_sin


def per_device(signals):
    seg_dev = signals.shape[2] // SEG_LEN
    parts = lax.axis_size("tm")
    x = signals.reshape(2, seg_dev, SEG_LEN // BLOCK, BLOCK)
    fars = jnp.stack([shifted(signals, "rx", step) for step in range(1, OFFS + 1)], axis=1)
    fars = fars.reshape(2, OFFS, seg_dev, SEG_LEN // BLOCK, BLOCK)
    half = BLOCK // 2
    table = jnp.asarray(forward_table())
    before = jnp.roll(x, 1, axis=2)[..., half:]
    after = jnp.roll(x, -1, axis=2)[..., :half]
    window = jnp.concatenate([before, x, after], axis=3)
    q = [v[None] for v in spectra(window, table)]
    p = spectra(fars, table[:BLOCK])
    pos_re = jnp.sum(q[0] * p[0] + q[1] * p[1], axis=2)
    pos_im = jnp.sum(q[1] * p[0] - q[0] * p[1], axis=2)
    neg_re = jnp.sum(q[2] * p[2] + q[3] * p[3], axis=2)
    neg_im = jnp.sum(q[3] * p[2] - q[2] * p[3], axis=2)
    even = jnp.concatenate([pos_re + neg_re, neg_im - pos_im], axis=2)
    odd = jnp.concatenate([pos_im + neg_im, pos_re - neg_re], axis=2)
    corr = jnp.dot(jnp.stack([even, odd]), jnp.asarray(inverse_table()), precision=PRECISION)
    blocks = jnp.moveaxis(corr.reshape(2, OFFS, seg_dev, parts, LAGS // parts), 3, 0)
    mine = lax.all_to_all(blocks, "tm", 0, 0, tiled=True)
    segs = parts * seg_dev
    rows = jnp.transpose(mine, (4, 2, 1, 0, 3)).reshape(LAGS // parts, OFFS, 2 * segs)
    out = jnp.dot(rows, jnp.asarray(doppler_table(segs)), precision=PRECISION)
    out = out.reshape(LAGS // parts, OFFS, 2, DOPK)
    return jnp.transpose(out, (0, 2, 1, 3))[:, :, None, :, None, :]


def solution(mesh):
    return jax.shard_map(
        per_device,
        mesh=mesh,
        in_specs=(P(None, "rx", "tm"),),
        out_specs=P("tm", None, "rx", None, None, None),
        check_vma=False,
    )
```

```python
import functools
import math

import jax
import jax.numpy as jnp
import ml_dtypes
import numpy as np
from jax import lax
from jax.experimental import pallas as pl
from jax.experimental.pallas import tpu as pltpu
from jax.sharding import PartitionSpec as P

SEG_LEN = 4096
LAGS = 256
DOPLEN = 512
DOPK = 256
OFFS = 4
WINDOW = 512
LANES = 128
GROUP = 4
SHARE = 4
UNITS = SEG_LEN // LANES
BLOCKS = SEG_LEN // 256
LAG_DEV = 32

MESH = pl.DeviceIdType.MESH

PAIRS = (
    ((0, 5), (1, 4)),
    ((0, 0), (1, 5), (2, 4)),
    ((0, 1), (1, 0), (2, 5), (3, 4)),
    ((0, 2), (1, 1), (2, 0), (3, 5)),
    ((2, 1), (3, 0)),
    ((3, 1),),
)


def split_table(table):
    table = table.astype(np.float32)
    high = table.astype(ml_dtypes.bfloat16)
    low = (table - high.astype(np.float32)).astype(ml_dtypes.bfloat16)
    return np.stack([high, low])


def forward_table():
    sample = np.arange(WINDOW)[:, None]
    freq = np.arange(WINDOW // 2)[None, :] + 0.5
    angle = 2.0 * np.pi / WINDOW * sample * freq
    return split_table(np.concatenate([np.cos(angle), np.sin(angle)], axis=1))


def inverse_table():
    lag = np.arange(LAGS)[None, :]
    freq = np.arange(WINDOW // 2)[:, None] + 0.5
    angle = 2.0 * np.pi / WINDOW * lag * freq
    return split_table(np.concatenate([np.cos(angle), np.sin(angle)], axis=0) / WINDOW)


def doppler_table(parts):
    seg = np.arange(parts * GROUP * SHARE).reshape(parts, GROUP, SHARE, 1)
    freq = np.arange(DOPK) - DOPK // 2
    angle = 2.0 * np.pi / DOPLEN * (seg * freq % DOPLEN)
    scale = 1.0 / math.sqrt(2.0 * SEG_LEN * parts * GROUP * SHARE)
    cos, sin = np.cos(angle) * scale, -np.sin(angle) * scale
    real_rows = np.concatenate([cos, sin], axis=-1)
    imag_rows = np.concatenate([-sin, cos], axis=-1)
    table = np.stack([real_rows, imag_rows], axis=2)
    return split_table(table.reshape(parts * GROUP * 2 * SHARE, 2 * DOPK))


def halves(value):
    high = value.astype(jnp.bfloat16)
    low = (value - high.astype(jnp.float32)).astype(jnp.bfloat16)
    return high, low


def product(value, high_table, low_table):
    rows = value.shape[0]
    high, low = halves(value)
    both = jnp.dot(
        jnp.concatenate([high, low], axis=0), high_table, preferred_element_type=jnp.float32
    )
    small = jnp.dot(high, low_table, preferred_element_type=jnp.float32)
    return both[:rows] + (both[rows:] + small)


def store_spectra(mixed, ref, slot):
    rows, half = mixed.shape[0] // 2, mixed.shape[1] // 2
    a_cos, a_sin = mixed[:rows, :half], mixed[:rows, half:]
    b_cos, b_sin = mixed[rows:, :half], mixed[rows:, half:]
    ref[slot, :, 0 * half : 1 * half] = a_cos + b_sin
    ref[slot, :, 1 * half : 2 * half] = b_cos - a_sin
    ref[slot, :, 2 * half : 3 * half] = a_cos - b_sin
    ref[slot, :, 3 * half : 4 * half] = b_cos + a_sin


def turned(value, steps):
    rows = value.shape[0]
    near = pltpu.roll(value, steps % rows, 0)
    far = pltpu.roll(value, (steps - BLOCKS if steps > 0 else steps + BLOCKS) % rows, 0)
    index = lax.broadcasted_iota(jnp.int32, value.shape, 0) % BLOCKS
    return jnp.where(index == (0 if steps > 0 else BLOCKS - 1), far, near)


def row_sums(values):
    index = lax.broadcasted_iota(jnp.int32, values[0].shape, 0)
    step = 1
    while len(values) > 1:
        first = index // step % 2 == 0
        values = [
            jnp.where(first, a, b) + pltpu.roll(jnp.where(first, b, a), step, 0)
            for a, b in zip(values[0::2], values[1::2])
        ]
        step *= 2
    return values[0]


def kernel(
    planes,
    parts,
    x_ref,
    fwd_hbm,
    inv_hbm,
    dop_hbm,
    out_ref,
    buf,
    qs,
    ps,
    srow,
    ct,
    rin,
    rlow,
    merged,
    fin,
    fwd,
    inv,
    dop,
    table_sem,
    send_plane,
    send_z,
    recv_x,
    send_c,
    recv_in,
    recv_low,
    send_t,
    recv_t,
):
    rx, tm = lax.axis_index("rx"), lax.axis_index("tm")
    count = planes * GROUP
    me = rx % GROUP
    base = rx - me
    share = SHARE * UNITS

    def other(k):
        return (me // 2 + k // 2) % 2 * 2 + (me % 2 + k % 2) % 2

    tables = [
        pltpu.make_async_copy(fwd_hbm, fwd, table_sem.at[0]),
        pltpu.make_async_copy(inv_hbm, inv, table_sem.at[1]),
        pltpu.make_async_copy(dop_hbm, dop, table_sem.at[2]),
    ]
    for copy in tables:
        copy.start()

    def part_of_x(index):
        return x_ref.at[:, pl.ds(pl.multiple_of(index * share, share), share), :]

    own = pltpu.make_async_copy(part_of_x(me), buf.at[me], recv_x.at[me])
    own.start()

    barrier = pltpu.get_barrier_semaphore()
    for k in range(1, GROUP):
        pl.semaphore_signal(barrier, 1, device_id=(base + other(k), tm), device_id_type=MESH)
    below = (base + count - GROUP) % count
    above = (base + GROUP) % count
    for j in range(GROUP):
        pl.semaphore_signal(barrier, 1, device_id=(below + j, tm), device_id_type=MESH)
    pl.semaphore_signal(barrier, 1, device_id=(above + me, tm), device_id_type=MESH)
    for k in range(1, parts):
        pl.semaphore_signal(barrier, 1, device_id=(rx, (tm + k) % parts), device_id_type=MESH)
    pl.semaphore_wait(barrier, GROUP - 1 + GROUP + 1 + parts - 1)

    def plane_copy(k):
        j = other(k)
        return pltpu.make_async_remote_copy(
            src_ref=part_of_x(j),
            dst_ref=buf.at[me],
            send_sem=send_plane.at[k - 1],
            recv_sem=recv_x.at[me],
            device_id=(base + j, tm),
            device_id_type=MESH,
        )

    def z_copy(k, src):
        j = other(k)
        return pltpu.make_async_remote_copy(
            src_ref=src,
            dst_ref=buf.at[GROUP + j],
            send_sem=send_z.at[k],
            recv_sem=recv_x.at[GROUP + j],
            device_id=((rx + count + (j // 2 * 2 - 1) * GROUP) % count, tm),
            device_id_type=MESH,
        )

    def arrival(slot):
        return pltpu.make_async_remote_copy(
            src_ref=buf.at[slot],
            dst_ref=buf.at[slot],
            send_sem=send_z.at[0],
            recv_sem=recv_x.at[slot],
            device_id=(rx, tm),
            device_id_type=MESH,
        )

    for k in (3, 2, 1):
        plane_copy(k).start()
    z_copy(0, part_of_x(me)).start()
    tables[0].wait()

    def pieces(slot, comp):
        rows = buf.at[slot, comp]
        even = rows[pl.ds(0, share // 2, stride=2), :]
        odd = rows[pl.ds(1, share // 2, stride=2), :]
        return even, odd

    def window_spectra(slot, target):
        rows = []
        for comp in range(2):
            even, odd = pieces(slot, comp)
            rows.append(jnp.concatenate([turned(odd, 1), even, odd, turned(even, -1)], axis=1))
        mixed = product(jnp.concatenate(rows, axis=0), fwd[0], fwd[1])
        store_spectra(mixed, qs, target)

    def block_spectra(slot, target):
        rows = [jnp.concatenate(pieces(slot, comp), axis=1) for comp in range(2)]
        mixed = product(
            jnp.concatenate(rows, axis=0), fwd[0, : WINDOW // 2], fwd[1, : WINDOW // 2]
        )
        store_spectra(mixed, ps, target)

    def plane_step(k, carry):
        j = other(k)

        @pl.when(k == 0)
        def _():
            own.wait()

        @pl.when(k > 0)
        def _():
            arrival(j).wait_recv()
            z_copy(k, buf.at[j]).start()

        window_spectra(j, j)
        block_spectra(j, j)
        return carry

    lax.fori_loop(0, GROUP, plane_step, 0)

    def z_step(k, carry):
        j = other(k)
        arrival(GROUP + j).wait_recv()

        @pl.when(j < 2)
        def _():
            window_spectra(GROUP + j, GROUP + j)

        @pl.when(j >= 2)
        def _():
            block_spectra(GROUP + j, GROUP + j - 2)

        return carry

    lax.fori_loop(0, GROUP, z_step, 0)

    def half_step(half, carry):
        def part(ref, slot, seg, index):
            start = pl.multiple_of(index * (WINDOW // 2) + half * LANES, LANES)
            return ref[slot, seg * BLOCKS : (seg + 1) * BLOCKS, pl.ds(start, LANES)]

        pair = 0
        for slot, partners in enumerate(PAIRS):
            for _, far in partners:
                sums = []
                for seg in range(SHARE):
                    q = [part(qs, slot, seg, i) for i in range(4)]
                    p = [part(ps, far, seg, i) for i in range(4)]
                    z = [
                        q[0] * p[0] + q[1] * p[1],
                        q[1] * p[0] - q[0] * p[1],
                        q[2] * p[2] + q[3] * p[3],
                        q[3] * p[2] - q[2] * p[3],
                    ]
                    z = [v[:8] + v[8:] for v in z]
                    sums.append([z[0] + z[2], z[3] - z[1], z[1] + z[3], z[0] - z[2]])
                for i in range(2):
                    rows = [v[i] for v in sums] + [v[2 + i] for v in sums]
                    start = pl.multiple_of(i * (WINDOW // 2) + half * LANES, LANES)
                    srow[pair * 8 : pair * 8 + 8, pl.ds(start, LANES)] = row_sums(rows)
                pair += 1
        return carry

    lax.fori_loop(0, 2, half_step, 0)

    tables[1].wait()
    corr = product(srow[...], inv[0], inv[1])
    lane = lax.broadcasted_iota(jnp.int32, (8, LANES), 1)
    pair = 0
    for slot, partners in enumerate(PAIRS):
        for part in range(parts):
            col, piece = part // 4, part % 4
            tile = jnp.zeros((8, LANES), jnp.float32)
            for index, (off, _) in enumerate(partners):
                row = (pair + index) * 8
                value = corr[row : row + 8, col * LANES : (col + 1) * LANES]
                shift = LAG_DEV * (off - piece) % LANES
                if shift:
                    value = pltpu.roll(value, shift, 1)
                tile = jnp.where(lane // LAG_DEV == off, value, tile)
            ct[slot, part] = tile
        pair += len(partners)

    def corr_copy(k):
        j = other(k)
        return pltpu.make_async_remote_copy(
            src_ref=ct.at[j],
            dst_ref=rin.at[me],
            send_sem=send_c.at[k - 1],
            recv_sem=recv_in.at[me],
            device_id=(base + j, tm),
            device_id_type=MESH,
        )

    def low_copy(i):
        return pltpu.make_async_remote_copy(
            src_ref=ct.at[GROUP + i],
            dst_ref=rlow.at[me],
            send_sem=send_c.at[GROUP - 1 + i],
            recv_sem=recv_low.at[me],
            device_id=(above + i, tm),
            device_id_type=MESH,
        )

    for i in range(2):
        low_copy(i).start()
    for k in (3, 2, 1):
        corr_copy(k).start()
    own_c = pltpu.make_async_copy(ct.at[me], rin.at[me], recv_in.at[me])
    own_c.start()
    own_c.wait()

    def corr_arrival(ref, sems, slot):
        return pltpu.make_async_remote_copy(
            src_ref=ref.at[slot],
            dst_ref=ref.at[slot],
            send_sem=send_c.at[0],
            recv_sem=sems.at[slot],
            device_id=(rx, tm),
            device_id_type=MESH,
        )

    for k in range(1, GROUP):
        corr_arrival(rin, recv_in, other(k)).wait_recv()

    @pl.when(me < 2)
    def _():
        for slot in range(GROUP):
            corr_arrival(rlow, recv_low, slot).wait_recv()

    kept = lane < 2 * LAG_DEV + LAG_DEV * me
    for part in range(parts):
        for slot in range(GROUP):
            merged[part, slot * 8 : slot * 8 + 8] = jnp.where(
                kept, rin[slot, part], rlow[slot, part]
            )

    def lag_copy(k):
        to = (tm + k) % parts
        return pltpu.make_async_remote_copy(
            src_ref=merged.at[to],
            dst_ref=fin.at[tm],
            send_sem=send_t.at[k - 1],
            recv_sem=recv_t.at[k - 1],
            device_id=(rx, to),
            device_id_type=MESH,
        )

    for k in range(1, parts):
        lag_copy(k).start()
    fin[tm] = merged[tm]
    tables[2].wait()
    for k in range(1, parts):
        source = (tm + parts - k) % parts
        pltpu.make_async_remote_copy(
            src_ref=fin.at[source],
            dst_ref=fin.at[source],
            send_sem=send_t.at[k - 1],
            recv_sem=recv_t.at[k - 1],
            device_id=(rx, tm),
            device_id_type=MESH,
        ).wait_recv()

    columns = fin[...].reshape(parts * GROUP * 2 * SHARE, LANES)
    result = product(columns.T, dop[0], dop[1])
    for off in range(OFFS):
        for col in range(4):
            out_ref[pl.ds(col // 2 * 8 + off * 2 + col % 2, LAG_DEV, stride=16), :] = result[
                off * LAG_DEV : (off + 1) * LAG_DEV, col * LANES : (col + 1) * LANES
            ]

    for k in range(1, GROUP):
        plane_copy(k).wait_send()
        corr_copy(k).wait_send()
    for k in range(GROUP):
        z_copy(k, buf.at[0]).wait_send()
    for i in range(2):
        low_copy(i).wait_send()
    for k in range(1, parts):
        lag_copy(k).wait_send()


def per_device(planes, parts, signals):
    rows = signals.reshape(2, -1, LANES)
    dop_rows = parts * GROUP * 2 * SHARE
    dma, vmem = pltpu.SemaphoreType.DMA, pltpu.VMEM
    out = pl.pallas_call(
        functools.partial(kernel, planes, parts),
        out_shape=jax.ShapeDtypeStruct((LAG_DEV * 2 * OFFS * 2, LANES), jnp.float32),
        in_specs=[pl.BlockSpec(memory_space=pl.ANY)] * 4,
        out_specs=pl.BlockSpec(memory_space=pltpu.VMEM),
        scratch_shapes=[
            vmem((2 * GROUP, 2, SHARE * UNITS, LANES), jnp.float32),
            vmem((6, SHARE * BLOCKS, 2 * WINDOW), jnp.float32),
            vmem((6, SHARE * BLOCKS, 2 * WINDOW), jnp.float32),
            vmem((16 * 8, WINDOW), jnp.float32),
            vmem((6, parts, 8, LANES), jnp.float32),
            vmem((GROUP, parts, 8, LANES), jnp.float32),
            vmem((GROUP, parts, 8, LANES), jnp.float32),
            vmem((parts, GROUP * 8, LANES), jnp.float32),
            vmem((parts, GROUP * 8, LANES), jnp.float32),
            vmem((2, WINDOW, WINDOW), jnp.bfloat16),
            vmem((2, WINDOW, LAGS), jnp.bfloat16),
            vmem((2, dop_rows, 2 * DOPK), jnp.bfloat16),
            dma((3,)),
            dma((GROUP - 1,)),
            dma((GROUP,)),
            dma((2 * GROUP,)),
            dma((GROUP + 1,)),
            dma((GROUP,)),
            dma((GROUP,)),
            dma((parts - 1,)),
            dma((parts - 1,)),
        ],
        compiler_params=pltpu.CompilerParams(
            collective_id=0, has_side_effects=True, vmem_limit_bytes=48 * 1024 * 1024
        ),
        name="ambiguity",
    )(
        rows,
        jnp.asarray(forward_table()),
        jnp.asarray(inverse_table()),
        jnp.asarray(doppler_table(parts)),
    )
    return out.reshape(LAG_DEV, 2, 1, OFFS, 1, DOPK)


def solution(mesh):
    planes, parts = mesh.shape["rx"] // GROUP, mesh.shape["tm"]
    return jax.shard_map(
        functools.partial(per_device, planes, parts),
        mesh=mesh,
        in_specs=(P(None, "rx", "tm"),),
        out_specs=P("tm", None, "rx", None, None, None),
        check_vma=False,
    )
```

```python
import functools
import math

import jax
import jax.numpy as jnp
import ml_dtypes
import numpy as np
from jax import lax
from jax.experimental import pallas as pl
from jax.experimental.pallas import tpu as pltpu
from jax.sharding import PartitionSpec as P

SEG_LEN = 4096
LAGS = 256
DOPLEN = 512
DOPK = 256
OFFS = 4
WINDOW = 512
LANES = 128
GROUP = 4
SHARE = 4
UNITS = SEG_LEN // LANES
BLOCKS = SEG_LEN // 256
LAG_DEV = 32
VMEM_LIMIT = 67043328 - 384 * 1024

MESH = pl.DeviceIdType.MESH

PAIRS = (
    ((0, 5), (1, 4)),
    ((0, 0), (1, 5), (2, 4)),
    ((0, 1), (1, 0), (2, 5), (3, 4)),
    ((0, 2), (1, 1), (2, 0), (3, 5)),
    ((2, 1), (3, 0)),
    ((3, 1),),
)


def split_table(table):
    table = table.astype(np.float32)
    high = table.astype(ml_dtypes.bfloat16)
    low = (table - high.astype(np.float32)).astype(ml_dtypes.bfloat16)
    return np.stack([high, low])


def forward_table():
    sample = np.arange(WINDOW)[:, None]
    freq = np.arange(WINDOW // 2)[None, :] + 0.5
    angle = 2.0 * np.pi / WINDOW * sample * freq
    return split_table(np.concatenate([np.cos(angle), np.sin(angle)], axis=1))


def inverse_table():
    lag = np.arange(LAGS)[None, :]
    freq = np.arange(WINDOW // 2)[:, None] + 0.5
    angle = 2.0 * np.pi / WINDOW * lag * freq
    return split_table(np.concatenate([np.cos(angle), np.sin(angle)], axis=0) / WINDOW)


def doppler_table(parts):
    seg = np.arange(parts * GROUP * SHARE).reshape(parts, GROUP, SHARE, 1)
    freq = np.arange(DOPK) - DOPK // 2
    angle = 2.0 * np.pi / DOPLEN * (seg * freq % DOPLEN)
    scale = 1.0 / math.sqrt(2.0 * SEG_LEN * parts * GROUP * SHARE)
    cos, sin = np.cos(angle) * scale, -np.sin(angle) * scale
    real_rows = np.concatenate([cos, sin], axis=-1)
    imag_rows = np.concatenate([-sin, cos], axis=-1)
    table = np.stack([real_rows, imag_rows], axis=3)
    return split_table(table.reshape(parts * GROUP * 2 * SHARE, 2 * DOPK))


def halves(value):
    high = value.astype(jnp.bfloat16)
    low = (value - high.astype(jnp.float32)).astype(jnp.bfloat16)
    return high, low


def product(value, high_table, low_table):
    rows = value.shape[0]
    high, low = halves(value)
    both = jnp.dot(
        jnp.concatenate([high, low], axis=0), high_table, preferred_element_type=jnp.float32
    )
    small = jnp.dot(high, low_table, preferred_element_type=jnp.float32)
    return both[:rows] + (both[rows:] + small)


def store_spectra(mixed, ref, side, start):
    rows, half = mixed.shape[0] // 2, mixed.shape[1] // 2
    a_cos, a_sin = mixed[:rows, :half], mixed[:rows, half:]
    b_cos, b_sin = mixed[rows:, :half], mixed[rows:, half:]
    parts = (a_cos + b_sin, b_cos - a_sin, a_cos - b_sin, b_cos + a_sin)
    for index, part in enumerate(parts):
        ref[side, start : start + rows, index * half : (index + 1) * half] = part


def row_sums(values):
    index = lax.broadcasted_iota(jnp.int32, values[0].shape, 0)
    step = 1
    while len(values) > 1:
        first = index // step % 2 == 0
        values = [
            jnp.where(first, a, b) + pltpu.roll(jnp.where(first, b, a), step, 0)
            for a, b in zip(values[0::2], values[1::2])
        ]
        step *= 2
    return values[0]


def kernel(
    planes,
    parts,
    x_ref,
    fwd_hbm,
    inv_hbm,
    dop_hbm,
    out_ref,
    buf,
    qs,
    ps,
    srow,
    corr,
    ct,
    fin,
    low,
    fwd,
    inv,
    dop,
    table_sem,
    send_plane,
    send_z,
    recv_x,
    send_c,
    recv_c,
):
    rx, tm = lax.axis_index("rx"), lax.axis_index("tm")
    count = planes * GROUP
    me = rx % GROUP
    base = rx - me
    below = (base + count - GROUP) % count
    above = (base + GROUP) % count

    def other(k):
        return (me // 2 + k // 2) % 2 * 2 + (me % 2 + k % 2) % 2

    def part_of_x(index, seg):
        start = pl.multiple_of((index * SHARE + seg) * UNITS, UNITS)
        return x_ref.at[:, pl.ds(start, UNITS), :]

    def own_copy(seg):
        return pltpu.make_async_copy(part_of_x(me, seg), buf.at[me, seg], recv_x.at[me, seg])

    def plane_copy(k, seg):
        j = other(k)
        return pltpu.make_async_remote_copy(
            src_ref=part_of_x(j, seg),
            dst_ref=buf.at[me, seg],
            send_sem=send_plane.at[k - 1, seg],
            recv_sem=recv_x.at[me, seg],
            device_id=(base + j, tm),
            device_id_type=MESH,
        )

    def z_copy(k, seg, src):
        j = other(k)
        return pltpu.make_async_remote_copy(
            src_ref=src,
            dst_ref=buf.at[GROUP + j, seg],
            send_sem=send_z.at[k, seg],
            recv_sem=recv_x.at[GROUP + j, seg],
            device_id=((rx + count + (j // 2 * 2 - 1) * GROUP) % count, tm),
            device_id_type=MESH,
        )

    def received(ref, sem):
        return pltpu.make_async_remote_copy(
            src_ref=ref,
            dst_ref=ref,
            send_sem=send_c.at[0],
            recv_sem=sem,
            device_id=(rx, tm),
            device_id_type=MESH,
        )

    tables = [
        pltpu.make_async_copy(fwd_hbm, fwd, table_sem.at[0]),
        pltpu.make_async_copy(inv_hbm, inv, table_sem.at[1]),
        pltpu.make_async_copy(dop_hbm, dop, table_sem.at[2]),
    ]

    barrier = pltpu.get_barrier_semaphore()

    def greet(r, t):
        pl.semaphore_signal(barrier, 1, device_id=(r, t), device_id_type=MESH)

    greet(below + me, tm)
    greet(above + me, tm)
    for k in range(GROUP):
        for step in range(parts):
            if k or step:
                greet(base + other(k), (tm + step) % parts)

    @pl.when(me < 2)
    def _():
        for k in range(GROUP):
            for step in range(parts):
                greet(below + other(k), (tm + step) % parts)

    for copy in tables:
        copy.start()
    for seg in range(SHARE):
        own_copy(seg).start()
    pl.semaphore_wait(barrier, 2 + GROUP * parts - 1 + 2 * parts)

    for seg in range(SHARE):
        for k in (3, 2, 1):
            plane_copy(k, seg).start()
        z_copy(0, seg, part_of_x(me, seg)).start()
    tables[0].wait()

    def pieces(slot, seg, comp):
        rows = buf.at[slot, seg, comp]
        even = rows[pl.ds(0, BLOCKS, stride=2), :]
        odd = rows[pl.ds(1, BLOCKS, stride=2), :]
        return even, odd

    def window(slot, seg, comp):
        even, odd = pieces(slot, seg, comp)
        before = pltpu.roll(odd, 1, 0)
        after = pltpu.roll(even, BLOCKS - 1, 0)
        return jnp.concatenate([before, even, odd, after], axis=1)

    def window_spectra(slots, seg, side):
        rows = [window(slot, seg, comp) for comp in range(2) for slot in slots]
        mixed = product(jnp.concatenate(rows, axis=0), fwd[0], fwd[1])
        store_spectra(mixed, qs, side, slots[0] * BLOCKS)

    def block_spectra(slots, seg, side, target):
        rows = [
            jnp.concatenate(pieces(slot, seg, comp), axis=1) for comp in range(2) for slot in slots
        ]
        mixed = product(
            jnp.concatenate(rows, axis=0), fwd[0, : WINDOW // 2], fwd[1, : WINDOW // 2]
        )
        store_spectra(mixed, ps, side, target * BLOCKS)

    order = [(slot, off, far) for slot, partners in enumerate(PAIRS) for off, far in partners]

    def correlate(seg, side):
        def half_step(half, carry):
            def part(ref, slot, index):
                start = pl.multiple_of(index * (WINDOW // 2) + half * LANES, LANES)
                return ref[side, slot * BLOCKS : (slot + 1) * BLOCKS, pl.ds(start, LANES)]

            for group in range(2):
                sums = []
                for slot, _, far in order[group * 8 : group * 8 + 8]:
                    q = [part(qs, slot, i) for i in range(4)]
                    p = [part(ps, far, i) for i in range(4)]
                    z = [
                        q[0] * p[0] + q[1] * p[1],
                        q[1] * p[0] - q[0] * p[1],
                        q[2] * p[2] + q[3] * p[3],
                        q[3] * p[2] - q[2] * p[3],
                    ]
                    z = [v[:8] + v[8:] for v in z]
                    sums.append([z[0] + z[2], z[3] - z[1], z[1] + z[3], z[0] - z[2]])
                for i in range(4):
                    row = pl.multiple_of(seg * 32 + i // 2 * 16 + group * 8, 8)
                    lane = pl.multiple_of(i % 2 * (WINDOW // 2) + half * LANES, LANES)
                    srow[pl.ds(row, 8), pl.ds(lane, LANES)] = row_sums([v[i] for v in sums])
            return carry

        lax.fori_loop(0, 2, half_step, 0)

    def seg_step(step, carry):
        @pl.when(step < SHARE)
        def _():
            for k in range(1, GROUP):
                j = other(k)
                received(buf.at[j, step], recv_x.at[j, step]).wait_recv()
                z_copy(k, step, buf.at[j, step]).start()
            own_copy(step).wait()
            window_spectra(range(0, 4), step, step % 2)
            block_spectra(range(0, 3), step, step % 2, 0)

        @pl.when(step > 0)
        def _():
            seg = step - 1
            for slot in range(GROUP, 2 * GROUP):
                received(buf.at[slot, seg], recv_x.at[slot, seg]).wait_recv()
            window_spectra(range(4, 6), seg, seg % 2)
            block_spectra(range(6, 8), seg, seg % 2, 4)
            correlate(seg, seg % 2)

        return carry

    lax.fori_loop(0, SHARE + 1, seg_step, 0)

    tables[1].wait()
    lags = product(srow[...], inv[0], inv[1])
    corr[0], corr[1] = lags[:, :LANES], lags[:, LANES:]
    lane = lax.broadcasted_iota(jnp.int32, (8, LANES), 1)
    for slot in range(6):
        for col in range(2):
            values = [
                (off, corr[col, pl.ds(index, 8, stride=16), :])
                for index, (at, off, _) in enumerate(order)
                if at == slot
            ]
            for piece in range(4):
                tile = jnp.zeros((8, LANES), jnp.float32)
                for off, value in values:
                    shift = LAG_DEV * (off - piece) % LANES
                    if shift:
                        value = pltpu.roll(value, shift, 1)
                    tile = jnp.where(lane // LAG_DEV == off, value, tile)
                if col * 4 + piece < parts:
                    ct[slot, col * 4 + piece] = tile

    def tile_copy(k, step):
        j, to = other(k), (tm + step) % parts
        return pltpu.make_async_remote_copy(
            src_ref=ct.at[j, to],
            dst_ref=fin.at[tm, me],
            send_sem=send_c.at[min(k, 1)],
            recv_sem=recv_c.at[min(k, 1)],
            device_id=(base + j, to),
            device_id_type=MESH,
        )

    def low_copy(i, step):
        to = (tm + step) % parts
        return pltpu.make_async_remote_copy(
            src_ref=ct.at[GROUP + i, to],
            dst_ref=low.at[tm, me],
            send_sem=send_c.at[2],
            recv_sem=recv_c.at[2],
            device_id=(above + i, to),
            device_id_type=MESH,
        )

    for step in range(parts):
        for i in range(2):
            low_copy(i, step).start()
        for k in (3, 2, 1, 0):
            if k or step:
                tile_copy(k, step).start()
    fin[tm, me] = ct[me, tm]
    tables[2].wait()

    @pl.when(me < 2)
    def _():
        received(low, recv_c.at[2]).wait_recv()

    received(fin.at[:, : GROUP - 1], recv_c.at[1]).wait_recv()
    received(fin.at[: parts - 1, 0], recv_c.at[0]).wait_recv()

    rows = parts * GROUP * 2 * SHARE
    lanes = lax.broadcasted_iota(jnp.int32, (rows, LANES), 1)
    columns = jnp.where(
        lanes < 2 * LAG_DEV + LAG_DEV * me,
        fin[...].reshape(rows, LANES),
        low[...].reshape(rows, LANES),
    )
    result = product(columns.T, dop[0], dop[1])
    for off in range(OFFS):
        for col in range(4):
            out_ref[pl.ds(col // 2 * 8 + off * 2 + col % 2, LAG_DEV, stride=16), :] = result[
                off * LAG_DEV : (off + 1) * LAG_DEV, col * LANES : (col + 1) * LANES
            ]

    for seg in range(SHARE):
        for k in range(GROUP):
            if k:
                plane_copy(k, seg).wait_send()
            z_copy(k, seg, buf.at[0, seg]).wait_send()

    def sent(ref, sem):
        pltpu.make_async_remote_copy(
            src_ref=ref,
            dst_ref=ref,
            send_sem=sem,
            recv_sem=recv_c.at[0],
            device_id=(rx, tm),
            device_id_type=MESH,
        ).wait_send()

    sent(ct.at[0, : parts - 1], send_c.at[0])
    sent(ct.at[: GROUP - 1], send_c.at[1])
    sent(ct.at[GROUP : GROUP + 2], send_c.at[2])


def per_device(planes, parts, signals):
    rows = signals.reshape(2, -1, LANES)
    dop_rows = parts * GROUP * 2 * SHARE
    dma, vmem = pltpu.SemaphoreType.DMA, pltpu.VMEM
    out = pl.pallas_call(
        functools.partial(kernel, planes, parts),
        out_shape=jax.ShapeDtypeStruct((LAG_DEV * 2 * OFFS * 2, LANES), jnp.float32),
        in_specs=[pl.BlockSpec(memory_space=pl.ANY)] * 4,
        out_specs=pl.BlockSpec(memory_space=pltpu.VMEM),
        scratch_shapes=[
            vmem((2 * GROUP, SHARE, 2, UNITS, LANES), jnp.float32),
            vmem((2, 6 * BLOCKS, 2 * WINDOW), jnp.float32),
            vmem((2, 6 * BLOCKS, 2 * WINDOW), jnp.float32),
            vmem((SHARE * 32, WINDOW), jnp.float32),
            vmem((2, SHARE * 32, LANES), jnp.float32),
            vmem((6, parts, 8, LANES), jnp.float32),
            vmem((parts, GROUP, 8, LANES), jnp.float32),
            vmem((parts, GROUP, 8, LANES), jnp.float32),
            vmem((2, WINDOW, WINDOW), jnp.bfloat16),
            vmem((2, WINDOW, LAGS), jnp.bfloat16),
            vmem((2, dop_rows, 2 * DOPK), jnp.bfloat16),
            dma((3,)),
            dma((GROUP - 1, SHARE)),
            dma((GROUP, SHARE)),
            dma((2 * GROUP, SHARE)),
            dma((3,)),
            dma((3,)),
        ],
        compiler_params=pltpu.CompilerParams(
            collective_id=0, has_side_effects=True, vmem_limit_bytes=VMEM_LIMIT
        ),
        name="ambiguity",
    )(
        rows,
        jnp.asarray(forward_table()),
        jnp.asarray(inverse_table()),
        jnp.asarray(doppler_table(parts)),
    )
    return out.reshape(LAG_DEV, 2, 1, OFFS, 1, DOPK)


def solution(mesh):
    planes, parts = mesh.shape["rx"] // GROUP, mesh.shape["tm"]
    return jax.shard_map(
        functools.partial(per_device, planes, parts),
        mesh=mesh,
        in_specs=(P(None, "rx", "tm"),),
        out_specs=P("tm", None, "rx", None, None, None),
        check_vma=False,
    )
```

```python
import functools
import math

import jax
import jax.numpy as jnp
import ml_dtypes
import numpy as np
from jax import lax
from jax.experimental import pallas as pl
from jax.experimental.pallas import tpu as pltpu
from jax.sharding import PartitionSpec as P

SEG_LEN = 4096
LAGS = 256
DOPLEN = 512
DOPK = 256
OFFS = 4
WINDOW = 512
LANES = 128
GROUP = 4
SHARE = 4
UNITS = SEG_LEN // LANES
BLOCKS = SEG_LEN // 256
LAG_DEV = 32
VMEM_LIMIT = 67043328 - 500 * 1024

MESH = pl.DeviceIdType.MESH

PAIRS = (
    ((0, 5), (1, 4)),
    ((0, 0), (1, 5), (2, 4)),
    ((0, 1), (1, 0), (2, 5), (3, 4)),
    ((0, 2), (1, 1), (2, 0), (3, 5)),
    ((2, 1), (3, 0)),
    ((3, 1),),
)


def split_table(table):
    table = table.astype(np.float32)
    high = table.astype(ml_dtypes.bfloat16)
    low = (table - high.astype(np.float32)).astype(ml_dtypes.bfloat16)
    return np.stack([high, low])


def forward_table():
    sample = np.arange(WINDOW)[:, None]
    freq = np.arange(WINDOW // 2)[None, :] + 0.5
    angle = 2.0 * np.pi / WINDOW * sample * freq
    return split_table(np.concatenate([np.cos(angle), np.sin(angle)], axis=1))


def inverse_table():
    lag = np.arange(LAGS)[None, :]
    freq = np.arange(WINDOW // 2)[:, None] + 0.5
    angle = 2.0 * np.pi / WINDOW * lag * freq
    return split_table(np.concatenate([np.cos(angle), np.sin(angle)], axis=0) / WINDOW)


def doppler_table(parts):
    seg = np.arange(parts * GROUP * SHARE).reshape(parts, GROUP, SHARE, 1)
    freq = np.arange(DOPK) - DOPK // 2
    angle = 2.0 * np.pi / DOPLEN * (seg * freq % DOPLEN)
    cos, sin = np.cos(angle), -np.sin(angle)
    real_rows = np.concatenate([cos, sin], axis=-1)
    imag_rows = np.concatenate([-sin, cos], axis=-1)
    table = np.stack([real_rows, imag_rows], axis=3)
    return split_table(table.reshape(parts * GROUP * 2 * SHARE, 2 * DOPK))


def halves(value):
    high = value.astype(jnp.bfloat16)
    low = (value - high.astype(jnp.float32)).astype(jnp.bfloat16)
    return high, low


def product(value, high_table, low_table):
    rows = value.shape[0]
    high, low = halves(value)
    both = jnp.dot(
        jnp.concatenate([high, low], axis=0), high_table, preferred_element_type=jnp.float32
    )
    small = jnp.dot(high, low_table, preferred_element_type=jnp.float32)
    return both[:rows] + (both[rows:] + small)


def store_spectra(mixed, ref, side, start):
    rows, half = mixed.shape[0] // 2, mixed.shape[1] // 2
    a_cos, a_sin = mixed[:rows, :half], mixed[:rows, half:]
    b_cos, b_sin = mixed[rows:, :half], mixed[rows:, half:]
    parts = (a_cos + b_sin, b_cos - a_sin, a_cos - b_sin, b_cos + a_sin)
    for index, part in enumerate(parts):
        ref[side, start : start + rows, index * half : (index + 1) * half] = part


def row_sums(values):
    index = lax.broadcasted_iota(jnp.int32, values[0].shape, 0)
    step = 1
    while len(values) > 1:
        first = index // step % 2 == 0
        values = [
            jnp.where(first, a, b) + pltpu.roll(jnp.where(first, b, a), step, 0)
            for a, b in zip(values[0::2], values[1::2])
        ]
        step *= 2
    return values[0]


def kernel(
    planes,
    parts,
    x_ref,
    fwd_hbm,
    inv_hbm,
    dop_hbm,
    out_ref,
    buf,
    qs,
    ps,
    srow,
    corr,
    ct,
    fin,
    low,
    fwd,
    inv,
    dop,
    table_sem,
    send_plane,
    send_z,
    recv_x,
    send_c,
    recv_c,
):
    rx, tm = lax.axis_index("rx"), lax.axis_index("tm")
    count = planes * GROUP
    me = rx % GROUP
    base = rx - me
    below = (base + count - GROUP) % count
    above = (base + GROUP) % count

    def other(k):
        return (me // 2 + k // 2) % 2 * 2 + (me % 2 + k % 2) % 2

    def part_of_x(index, seg):
        start = pl.multiple_of((index * SHARE + seg) * UNITS, UNITS)
        return x_ref.at[:, pl.ds(start, UNITS), :]

    def own_copy(seg):
        return pltpu.make_async_copy(part_of_x(me, seg), buf.at[me, seg], recv_x.at[me, seg])

    def plane_copy(k, seg):
        j = other(k)
        return pltpu.make_async_remote_copy(
            src_ref=part_of_x(j, seg),
            dst_ref=buf.at[me, seg],
            send_sem=send_plane.at[k - 1, seg],
            recv_sem=recv_x.at[me, seg],
            device_id=(base + j, tm),
            device_id_type=MESH,
        )

    def z_copy(k, seg, src):
        j = other(k)
        return pltpu.make_async_remote_copy(
            src_ref=src,
            dst_ref=buf.at[GROUP + j, seg],
            send_sem=send_z.at[k, seg],
            recv_sem=recv_x.at[GROUP + j, seg],
            device_id=((rx + count + (j // 2 * 2 - 1) * GROUP) % count, tm),
            device_id_type=MESH,
        )

    def received(ref, sem):
        return pltpu.make_async_remote_copy(
            src_ref=ref,
            dst_ref=ref,
            send_sem=send_c.at[0],
            recv_sem=sem,
            device_id=(rx, tm),
            device_id_type=MESH,
        )

    tables = [
        pltpu.make_async_copy(fwd_hbm, fwd, table_sem.at[0]),
        pltpu.make_async_copy(inv_hbm, inv, table_sem.at[1]),
        pltpu.make_async_copy(dop_hbm, dop, table_sem.at[2]),
    ]

    barrier = pltpu.get_barrier_semaphore()

    def greet(r, t):
        pl.semaphore_signal(barrier, 1, device_id=(r, t), device_id_type=MESH)

    greet(below + me, tm)
    greet(above + me, tm)
    for k in range(GROUP):
        for step in range(parts):
            if k or step:
                greet(base + other(k), (tm + step) % parts)

    @pl.when(me < 2)
    def _():
        for k in range(GROUP):
            for step in range(parts):
                greet(below + other(k), (tm + step) % parts)

    for copy in tables:
        copy.start()
    for seg in range(SHARE):
        own_copy(seg).start()
    pl.semaphore_wait(barrier, 2 + GROUP * parts - 1 + 2 * parts)

    for seg in range(SHARE):
        for k in (3, 2, 1):
            plane_copy(k, seg).start()
        z_copy(0, seg, part_of_x(me, seg)).start()
    tables[0].wait()

    def pieces(slot, seg, comp):
        rows = buf.at[slot, seg, comp]
        even = rows[pl.ds(0, BLOCKS, stride=2), :]
        odd = rows[pl.ds(1, BLOCKS, stride=2), :]
        return even, odd

    def window(slot, seg, comp):
        even, odd = pieces(slot, seg, comp)
        before = pltpu.roll(odd, 1, 0)
        after = pltpu.roll(even, BLOCKS - 1, 0)
        return jnp.concatenate([before, even, odd, after], axis=1)

    def window_spectra(slots, seg, side):
        rows = [window(slot, seg, comp) for comp in range(2) for slot in slots]
        mixed = product(jnp.concatenate(rows, axis=0), fwd[0], fwd[1])
        store_spectra(mixed, qs, side, slots[0] * BLOCKS)

    def block_spectra(slots, seg, side, target):
        rows = [
            jnp.concatenate(pieces(slot, seg, comp), axis=1) for comp in range(2) for slot in slots
        ]
        mixed = product(
            jnp.concatenate(rows, axis=0), fwd[0, : WINDOW // 2], fwd[1, : WINDOW // 2]
        )
        store_spectra(mixed, ps, side, target * BLOCKS)

    order = [(slot, off, far) for slot, partners in enumerate(PAIRS) for off, far in partners]

    def correlate(seg, side):
        def half_step(half, carry):
            def part(ref, slot, index):
                start = pl.multiple_of(index * (WINDOW // 2) + half * LANES, LANES)
                return ref[side, slot * BLOCKS : (slot + 1) * BLOCKS, pl.ds(start, LANES)]

            for group in range(2):
                sums = []
                for slot, _, far in order[group * 8 : group * 8 + 8]:
                    q = [part(qs, slot, i) for i in range(4)]
                    p = [part(ps, far, i) for i in range(4)]
                    z = [
                        q[0] * p[0] + q[1] * p[1],
                        q[1] * p[0] - q[0] * p[1],
                        q[2] * p[2] + q[3] * p[3],
                        q[3] * p[2] - q[2] * p[3],
                    ]
                    z = [v[:8] + v[8:] for v in z]
                    sums.append([z[0] + z[2], z[3] - z[1], z[1] + z[3], z[0] - z[2]])
                for i in range(4):
                    row = pl.multiple_of(seg * 32 + i // 2 * 16 + group * 8, 8)
                    lane = pl.multiple_of(i % 2 * (WINDOW // 2) + half * LANES, LANES)
                    srow[pl.ds(row, 8), pl.ds(lane, LANES)] = row_sums([v[i] for v in sums])
            return carry

        lax.fori_loop(0, 2, half_step, 0)

    def plane_step(seg, carry):
        for k in range(1, GROUP):
            j = other(k)
            received(buf.at[j, seg], recv_x.at[j, seg]).wait_recv()
            z_copy(k, seg, buf.at[j, seg]).start()
        own_copy(seg).wait()
        window_spectra(range(0, 4), seg, seg)
        block_spectra(range(0, 3), seg, seg, 0)
        return carry

    def z_step(seg, carry):
        for slot in range(GROUP, 2 * GROUP):
            received(buf.at[slot, seg], recv_x.at[slot, seg]).wait_recv()
        window_spectra(range(4, 6), seg, seg)
        block_spectra(range(6, 8), seg, seg, 4)
        correlate(seg, seg)
        return carry

    lax.fori_loop(0, SHARE, plane_step, 0)
    lax.fori_loop(0, SHARE, z_step, 0)

    tables[1].wait()
    lags = product(srow[...], inv[0], inv[1])
    corr[0], corr[1] = lags[:, :LANES], lags[:, LANES:]
    lane = lax.broadcasted_iota(jnp.int32, (8, LANES), 1)
    for slot in range(6):
        for col in range(2):
            values = [
                (off, corr[col, pl.ds(index, 8, stride=16), :])
                for index, (at, off, _) in enumerate(order)
                if at == slot
            ]
            for piece in range(4):
                tile = jnp.zeros((8, LANES), jnp.float32)
                for off, value in values:
                    shift = LAG_DEV * (off - piece) % LANES
                    if shift:
                        value = pltpu.roll(value, shift, 1)
                    tile = jnp.where(lane // LAG_DEV == off, value, tile)
                if col * 4 + piece < parts:
                    ct[slot, col * 4 + piece] = tile

    def tile_copy(k, step):
        j, to = other(k), (tm + step) % parts
        return pltpu.make_async_remote_copy(
            src_ref=ct.at[j, to],
            dst_ref=fin.at[tm, me],
            send_sem=send_c.at[min(k, 1)],
            recv_sem=recv_c.at[min(k, 1)],
            device_id=(base + j, to),
            device_id_type=MESH,
        )

    def low_copy(i, step):
        to = (tm + step) % parts
        return pltpu.make_async_remote_copy(
            src_ref=ct.at[GROUP + i, to],
            dst_ref=low.at[tm, me],
            send_sem=send_c.at[2],
            recv_sem=recv_c.at[2],
            device_id=(above + i, to),
            device_id_type=MESH,
        )

    for step in range(parts):
        for i in range(2):
            low_copy(i, step).start()
        for k in (3, 2, 1, 0):
            if k or step:
                tile_copy(k, step).start()
    fin[tm, me] = ct[me, tm]
    tables[2].wait()

    @pl.when(me < 2)
    def _():
        received(low, recv_c.at[2]).wait_recv()

    received(fin.at[:, : GROUP - 1], recv_c.at[1]).wait_recv()
    received(fin.at[: parts - 1, 0], recv_c.at[0]).wait_recv()

    rows = parts * GROUP * 2 * SHARE
    lanes = lax.broadcasted_iota(jnp.int32, (rows, LANES), 1)
    columns = jnp.where(
        lanes < 2 * LAG_DEV + LAG_DEV * me,
        fin[...].reshape(rows, LANES),
        low[...].reshape(rows, LANES),
    )
    result = product(columns.T, dop[0], dop[1])
    for off in range(OFFS):
        for col in range(4):
            out_ref[pl.ds(col // 2 * 8 + off * 2 + col % 2, LAG_DEV, stride=16), :] = result[
                off * LAG_DEV : (off + 1) * LAG_DEV, col * LANES : (col + 1) * LANES
            ]

    for seg in range(SHARE):
        for k in range(GROUP):
            if k:
                plane_copy(k, seg).wait_send()
            z_copy(k, seg, buf.at[0, seg]).wait_send()

    def sent(ref, sem):
        pltpu.make_async_remote_copy(
            src_ref=ref,
            dst_ref=ref,
            send_sem=sem,
            recv_sem=recv_c.at[0],
            device_id=(rx, tm),
            device_id_type=MESH,
        ).wait_send()

    sent(ct.at[0, : parts - 1], send_c.at[0])
    sent(ct.at[: GROUP - 1], send_c.at[1])
    sent(ct.at[GROUP : GROUP + 2], send_c.at[2])


def per_device(planes, parts, signals):
    rows = signals.reshape(2, -1, LANES)
    dop_rows = parts * GROUP * 2 * SHARE
    dma, vmem = pltpu.SemaphoreType.DMA, pltpu.VMEM
    out = pl.pallas_call(
        functools.partial(kernel, planes, parts),
        out_shape=jax.ShapeDtypeStruct((LAG_DEV * 2 * OFFS * 2, LANES), jnp.float32),
        in_specs=[pl.BlockSpec(memory_space=pl.ANY)] * 4,
        out_specs=pl.BlockSpec(memory_space=pltpu.VMEM),
        scratch_shapes=[
            vmem((2 * GROUP, SHARE, 2, UNITS, LANES), jnp.float32),
            vmem((SHARE, 6 * BLOCKS, 2 * WINDOW), jnp.float32),
            vmem((SHARE, 6 * BLOCKS, 2 * WINDOW), jnp.float32),
            vmem((SHARE * 32, WINDOW), jnp.float32),
            vmem((2, SHARE * 32, LANES), jnp.float32),
            vmem((6, parts, 8, LANES), jnp.float32),
            vmem((parts, GROUP, 8, LANES), jnp.float32),
            vmem((parts, GROUP, 8, LANES), jnp.float32),
            vmem((2, WINDOW, WINDOW), jnp.bfloat16),
            vmem((2, WINDOW, LAGS), jnp.bfloat16),
            vmem((2, dop_rows, 2 * DOPK), jnp.bfloat16),
            dma((3,)),
            dma((GROUP - 1, SHARE)),
            dma((GROUP, SHARE)),
            dma((2 * GROUP, SHARE)),
            dma((3,)),
            dma((3,)),
        ],
        compiler_params=pltpu.CompilerParams(
            collective_id=0, has_side_effects=True, vmem_limit_bytes=VMEM_LIMIT
        ),
        name="ambiguity",
    )(
        rows,
        jnp.asarray(forward_table()),
        jnp.asarray(inverse_table()),
        jnp.asarray(doppler_table(parts)),
    )
    scale = 1.0 / math.sqrt(2.0 * SEG_LEN * parts * GROUP * SHARE)
    return out.reshape(LAG_DEV, 2, 1, OFFS, 1, DOPK) * jnp.float32(scale)


def solution(mesh):
    planes, parts = mesh.shape["rx"] // GROUP, mesh.shape["tm"]
    return jax.shard_map(
        functools.partial(per_device, planes, parts),
        mesh=mesh,
        in_specs=(P(None, "rx", "tm"),),
        out_specs=P("tm", None, "rx", None, None, None),
        check_vma=False,
    )
```

```python
import functools
import math

import jax
import jax.numpy as jnp
import ml_dtypes
import numpy as np
from jax import lax
from jax.experimental import pallas as pl
from jax.experimental.pallas import tpu as pltpu
from jax.sharding import PartitionSpec as P

SEG_LEN = 4096
LAGS = 256
DOPLEN = 512
DOPK = 256
OFFS = 4
WINDOW = 512
LANES = 128
GROUP = 4
SHARE = 4
UNITS = SEG_LEN // LANES
BLOCKS = SEG_LEN // 256
LAG_DEV = 32
SPLIT = 2
CHUNKS = SHARE * SPLIT
LAG_STEPS = 2
CHUNK = UNITS // SPLIT
VMEM_LIMIT = 67043328 - 10800 * 1024

MESH = pl.DeviceIdType.MESH

PAIRS = (
    ((0, 5), (1, 4)),
    ((0, 0), (1, 5), (2, 4)),
    ((0, 1), (1, 0), (2, 5), (3, 4)),
    ((0, 2), (1, 1), (2, 0), (3, 5)),
    ((2, 1), (3, 0)),
    ((3, 1),),
)


def split_table(table):
    table = table.astype(np.float32)
    high = table.astype(ml_dtypes.bfloat16)
    low = (table - high.astype(np.float32)).astype(ml_dtypes.bfloat16)
    return np.stack([high, low])


def forward_table():
    sample = np.arange(WINDOW)[:, None]
    freq = np.arange(WINDOW // 2)[None, :] + 0.5
    angle = 2.0 * np.pi / WINDOW * sample * freq
    return split_table(np.concatenate([np.cos(angle), np.sin(angle)], axis=1))


def inverse_table():
    lag = np.arange(LAGS)[None, :]
    freq = np.arange(WINDOW // 2)[:, None] + 0.5
    angle = 2.0 * np.pi / WINDOW * lag * freq
    return split_table(np.concatenate([np.cos(angle), np.sin(angle)], axis=0) / WINDOW)


def doppler_table(parts):
    seg = np.arange(parts * GROUP * SHARE).reshape(parts, GROUP, SHARE, 1)
    freq = np.arange(DOPK) - DOPK // 2
    angle = 2.0 * np.pi / DOPLEN * (seg * freq % DOPLEN)
    cos, sin = np.cos(angle), -np.sin(angle)
    real_rows = np.concatenate([cos, sin], axis=-1)
    imag_rows = np.concatenate([-sin, cos], axis=-1)
    table = np.stack([real_rows, imag_rows], axis=3)
    return split_table(table.reshape(parts * GROUP * 2 * SHARE, 2 * DOPK))


def halves(value):
    high = value.astype(jnp.bfloat16)
    low = (value - high.astype(jnp.float32)).astype(jnp.bfloat16)
    return high, low


def product(value, high_table, low_table):
    rows = value.shape[0]
    high, low = halves(value)
    both = jnp.dot(
        jnp.concatenate([high, low], axis=0), high_table, preferred_element_type=jnp.float32
    )
    small = jnp.dot(high, low_table, preferred_element_type=jnp.float32)
    return both[:rows] + (both[rows:] + small)


def store_spectra(mixed, ref, side, start):
    rows, half = mixed.shape[0] // 2, mixed.shape[1] // 2
    a_cos, a_sin = mixed[:rows, :half], mixed[:rows, half:]
    b_cos, b_sin = mixed[rows:, :half], mixed[rows:, half:]
    parts = (a_cos + b_sin, b_cos - a_sin, a_cos - b_sin, b_cos + a_sin)
    for index, part in enumerate(parts):
        ref[side, start : start + rows, index * half : (index + 1) * half] = part


def row_sums(values):
    index = lax.broadcasted_iota(jnp.int32, values[0].shape, 0)
    step = 1
    while len(values) > 1:
        first = index // step % 2 == 0
        values = [
            jnp.where(first, a, b) + pltpu.roll(jnp.where(first, b, a), step, 0)
            for a, b in zip(values[0::2], values[1::2])
        ]
        step *= 2
    return values[0]


def kernel(
    planes,
    parts,
    x_ref,
    fwd_hbm,
    inv_hbm,
    dop_hbm,
    out_ref,
    buf,
    qs,
    ps,
    srow,
    corr,
    ct,
    fin,
    low,
    fwd,
    inv,
    dop,
    table_sem,
    send_plane,
    send_z,
    recv_x,
    send_c,
    recv_c,
    ready,
):
    rx, tm = lax.axis_index("rx"), lax.axis_index("tm")
    count = planes * GROUP
    me = rx % GROUP
    base = rx - me
    below = (base + count - GROUP) % count
    above = (base + GROUP) % count

    def other(k):
        return (me // 2 + k // 2) % 2 * 2 + (me % 2 + k % 2) % 2

    def part_of_x(index, chunk):
        start = pl.multiple_of((index * CHUNKS + chunk) * CHUNK, CHUNK)
        return x_ref.at[:, pl.ds(start, CHUNK), :]

    def place(slot, chunk):
        start = pl.multiple_of(chunk % SPLIT * CHUNK, CHUNK)
        return buf.at[slot, chunk // SPLIT, :, pl.ds(start, CHUNK), :]

    def own_copy(seg):
        start = pl.multiple_of((me * SHARE + seg) * UNITS, UNITS)
        return pltpu.make_async_copy(
            x_ref.at[:, pl.ds(start, UNITS), :], buf.at[me, seg], recv_x.at[me, seg]
        )

    def plane_copy(k, chunk):
        j = other(k)
        return pltpu.make_async_remote_copy(
            src_ref=part_of_x(j, chunk),
            dst_ref=place(me, chunk),
            send_sem=send_plane.at[k - 1, chunk],
            recv_sem=recv_x.at[me, chunk],
            device_id=(base + j, tm),
            device_id_type=MESH,
        )

    def z_copy(k, chunk, src):
        j = other(k)
        return pltpu.make_async_remote_copy(
            src_ref=src,
            dst_ref=place(GROUP + j, chunk),
            send_sem=send_z.at[k, chunk],
            recv_sem=recv_x.at[GROUP + j, chunk],
            device_id=((rx + count + (j // 2 * 2 - 1) * GROUP) % count, tm),
            device_id_type=MESH,
        )

    def received(ref, sem):
        return pltpu.make_async_remote_copy(
            src_ref=ref,
            dst_ref=ref,
            send_sem=send_c.at[0],
            recv_sem=sem,
            device_id=(rx, tm),
            device_id_type=MESH,
        )

    tables = [
        pltpu.make_async_copy(fwd_hbm, fwd, table_sem.at[0]),
        pltpu.make_async_copy(inv_hbm, inv, table_sem.at[1]),
        pltpu.make_async_copy(dop_hbm, dop, table_sem.at[2]),
    ]

    barrier = pltpu.get_barrier_semaphore()

    def greet(r, t):
        pl.semaphore_signal(barrier, 1, device_id=(r, t), device_id_type=MESH)

    greet(below + me, tm)
    greet(above + me, tm)
    for k in range(1, GROUP):
        greet(base + other(k), tm)
    for step in range(1, parts):
        greet(rx, (tm + step) % parts)
    for copy in tables:
        copy.start()
    for seg in range(SHARE):
        own_copy(seg).start()
    pl.semaphore_wait(barrier, 2 + GROUP - 1 + parts - 1)

    for chunk in range(CHUNKS):
        for k in (3, 2, 1):
            plane_copy(k, chunk).start()
        z_copy(0, chunk, part_of_x(me, chunk)).start()

    for k in range(1, GROUP):
        pl.semaphore_signal(ready.at[0], 1, device_id=(base + other(k), tm), device_id_type=MESH)
    pl.semaphore_signal(ready.at[1], 1, device_id=(above + me, tm), device_id_type=MESH)
    tables[0].wait()
    pl.semaphore_wait(ready.at[1], 1)

    @pl.when(me < 2)
    def _():
        for k in range(GROUP):
            to = below + other(k)
            pl.semaphore_signal(ready.at[2], 1, device_id=(to, tm), device_id_type=MESH)

    def pieces(slot, seg, comp):
        rows = buf.at[slot, seg, comp]
        even = rows[pl.ds(0, BLOCKS, stride=2), :]
        odd = rows[pl.ds(1, BLOCKS, stride=2), :]
        return even, odd

    def window(slot, seg, comp):
        even, odd = pieces(slot, seg, comp)
        before = pltpu.roll(odd, 1, 0)
        after = pltpu.roll(even, BLOCKS - 1, 0)
        return jnp.concatenate([before, even, odd, after], axis=1)

    def window_spectra(slots, seg, side):
        rows = [window(slot, seg, comp) for comp in range(2) for slot in slots]
        mixed = product(jnp.concatenate(rows, axis=0), fwd[0], fwd[1])
        store_spectra(mixed, qs, side, slots[0] * BLOCKS)

    def block_spectra(slots, seg, side, target):
        rows = [
            jnp.concatenate(pieces(slot, seg, comp), axis=1) for comp in range(2) for slot in slots
        ]
        mixed = product(
            jnp.concatenate(rows, axis=0), fwd[0, : WINDOW // 2], fwd[1, : WINDOW // 2]
        )
        store_spectra(mixed, ps, side, target * BLOCKS)

    order = [(slot, off, far) for slot, partners in enumerate(PAIRS) for off, far in partners]

    def correlate(seg, side):
        def half_step(half, carry):
            def part(ref, slot, index):
                start = pl.multiple_of(index * (WINDOW // 2) + half * LANES, LANES)
                return ref[side, slot * BLOCKS : (slot + 1) * BLOCKS, pl.ds(start, LANES)]

            for group in range(2):
                sums = []
                for slot, _, far in order[group * 8 : group * 8 + 8]:
                    q = [part(qs, slot, i) for i in range(4)]
                    p = [part(ps, far, i) for i in range(4)]
                    z = [
                        q[0] * p[0] + q[1] * p[1],
                        q[1] * p[0] - q[0] * p[1],
                        q[2] * p[2] + q[3] * p[3],
                        q[3] * p[2] - q[2] * p[3],
                    ]
                    z = [v[:8] + v[8:] for v in z]
                    sums.append([z[0] + z[2], z[3] - z[1], z[1] + z[3], z[0] - z[2]])
                for i in range(4):
                    row = pl.multiple_of(seg * 32 + i // 2 * 16 + group * 8, 8)
                    lane = pl.multiple_of(i % 2 * (WINDOW // 2) + half * LANES, LANES)
                    srow[pl.ds(row, 8), pl.ds(lane, LANES)] = row_sums([v[i] for v in sums])
            return carry

        lax.fori_loop(0, 2, half_step, 0)

    def arrived(slot, chunk):
        received(place(slot, chunk), recv_x.at[slot, chunk]).wait_recv()

    def seg_step(step, carry):
        @pl.when(step < SHARE)
        def _():
            for part in range(SPLIT):
                chunk = step * SPLIT + part
                for k in range(1, GROUP):
                    arrived(other(k), chunk)
                    z_copy(k, chunk, place(other(k), chunk)).start()
            own_copy(step).wait()
            window_spectra(range(0, 4), step, step)
            block_spectra(range(0, 3), step, step, 0)

        @pl.when(step >= LAG_STEPS)
        def _():
            seg = step - LAG_STEPS
            for part in range(SPLIT):
                for slot in range(GROUP, 2 * GROUP):
                    arrived(slot, seg * SPLIT + part)
            window_spectra(range(4, 6), seg, seg)
            block_spectra(range(6, 8), seg, seg, 4)
            correlate(seg, seg)

        return carry

    lax.fori_loop(0, SHARE + LAG_STEPS, seg_step, 0)

    tables[1].wait()
    lags = product(srow[...], inv[0], inv[1])
    corr[0], corr[1] = lags[:, :LANES], lags[:, LANES:]
    lane = lax.broadcasted_iota(jnp.int32, (8, LANES), 1)
    for slot in range(6):
        for col in range(2):
            values = [
                (off, corr[col, pl.ds(index, 8, stride=16), :])
                for index, (at, off, _) in enumerate(order)
                if at == slot
            ]
            for piece in range(4):
                tile = jnp.zeros((8, LANES), jnp.float32)
                for off, value in values:
                    shift = LAG_DEV * (off - piece) % LANES
                    if shift:
                        value = pltpu.roll(value, shift, 1)
                    tile = jnp.where(lane // LAG_DEV == off, value, tile)
                if col * 4 + piece < parts:
                    ct[slot, col * 4 + piece] = tile

    def tile_copy(k, step):
        j, to = other(k), (tm + step) % parts
        return pltpu.make_async_remote_copy(
            src_ref=ct.at[j, to],
            dst_ref=fin.at[tm, me],
            send_sem=send_c.at[min(k, 1)],
            recv_sem=recv_c.at[min(k, 1)],
            device_id=(base + j, to),
            device_id_type=MESH,
        )

    def low_copy(i, step):
        to = (tm + step) % parts
        return pltpu.make_async_remote_copy(
            src_ref=ct.at[GROUP + i, to],
            dst_ref=low.at[tm, me],
            send_sem=send_c.at[2],
            recv_sem=recv_c.at[2],
            device_id=(above + i, to),
            device_id_type=MESH,
        )

    pl.semaphore_wait(ready.at[0], GROUP - 1)
    pl.semaphore_wait(ready.at[2], 2)
    for step in range(parts):
        for i in range(2):
            low_copy(i, step).start()
        for k in (3, 2, 1, 0):
            if k or step:
                tile_copy(k, step).start()
    fin[tm, me] = ct[me, tm]
    tables[2].wait()

    @pl.when(me < 2)
    def _():
        received(low, recv_c.at[2]).wait_recv()

    received(fin.at[:, : GROUP - 1], recv_c.at[1]).wait_recv()
    received(fin.at[: parts - 1, 0], recv_c.at[0]).wait_recv()

    rows = parts * GROUP * 2 * SHARE
    lanes = lax.broadcasted_iota(jnp.int32, (rows, LANES), 1)
    columns = jnp.where(
        lanes < 2 * LAG_DEV + LAG_DEV * me,
        fin[...].reshape(rows, LANES),
        low[...].reshape(rows, LANES),
    )
    result = product(columns.T, dop[0], dop[1])
    for off in range(OFFS):
        for col in range(4):
            out_ref[pl.ds(col // 2 * 8 + off * 2 + col % 2, LAG_DEV, stride=16), :] = result[
                off * LAG_DEV : (off + 1) * LAG_DEV, col * LANES : (col + 1) * LANES
            ]

    for chunk in range(CHUNKS):
        for k in range(GROUP):
            if k:
                plane_copy(k, chunk).wait_send()
            z_copy(k, chunk, part_of_x(me, chunk)).wait_send()

    def sent(ref, sem):
        pltpu.make_async_remote_copy(
            src_ref=ref,
            dst_ref=ref,
            send_sem=sem,
            recv_sem=recv_c.at[0],
            device_id=(rx, tm),
            device_id_type=MESH,
        ).wait_send()

    sent(ct.at[0, : parts - 1], send_c.at[0])
    sent(ct.at[: GROUP - 1], send_c.at[1])
    sent(ct.at[GROUP : GROUP + 2], send_c.at[2])


def per_device(planes, parts, signals):
    rows = signals.reshape(2, -1, LANES)
    dop_rows = parts * GROUP * 2 * SHARE
    dma, vmem = pltpu.SemaphoreType.DMA, pltpu.VMEM
    out = pl.pallas_call(
        functools.partial(kernel, planes, parts),
        out_shape=jax.ShapeDtypeStruct((LAG_DEV * 2 * OFFS * 2, LANES), jnp.float32),
        in_specs=[pl.BlockSpec(memory_space=pl.ANY)] * 4,
        out_specs=pl.BlockSpec(memory_space=pltpu.VMEM),
        scratch_shapes=[
            vmem((2 * GROUP, SHARE, 2, UNITS, LANES), jnp.float32),
            vmem((SHARE, 6 * BLOCKS, 2 * WINDOW), jnp.float32),
            vmem((SHARE, 6 * BLOCKS, 2 * WINDOW), jnp.float32),
            vmem((SHARE * 32, WINDOW), jnp.float32),
            vmem((2, SHARE * 32, LANES), jnp.float32),
            vmem((6, parts, 8, LANES), jnp.float32),
            vmem((parts, GROUP, 8, LANES), jnp.float32),
            vmem((parts, GROUP, 8, LANES), jnp.float32),
            vmem((2, WINDOW, WINDOW), jnp.bfloat16),
            vmem((2, WINDOW, LAGS), jnp.bfloat16),
            vmem((2, dop_rows, 2 * DOPK), jnp.bfloat16),
            dma((3,)),
            dma((GROUP - 1, CHUNKS)),
            dma((GROUP, CHUNKS)),
            dma((2 * GROUP, CHUNKS)),
            dma((3,)),
            dma((3,)),
            pltpu.SemaphoreType.REGULAR((3,)),
        ],
        compiler_params=pltpu.CompilerParams(
            collective_id=0, has_side_effects=True, vmem_limit_bytes=VMEM_LIMIT
        ),
        name="ambiguity",
    )(
        rows,
        jnp.asarray(forward_table()),
        jnp.asarray(inverse_table()),
        jnp.asarray(doppler_table(parts)),
    )
    scale = 1.0 / math.sqrt(2.0 * SEG_LEN * parts * GROUP * SHARE)
    return out.reshape(LAG_DEV, 2, 1, OFFS, 1, DOPK) * jnp.float32(scale)


def solution(mesh):
    planes, parts = mesh.shape["rx"] // GROUP, mesh.shape["tm"]
    return jax.shard_map(
        functools.partial(per_device, planes, parts),
        mesh=mesh,
        in_specs=(P(None, "rx", "tm"),),
        out_specs=P("tm", None, "rx", None, None, None),
        check_vma=False,
    )
```

```python
import functools
import math

import jax
import jax.numpy as jnp
import ml_dtypes
import numpy as np
from jax import lax
from jax.experimental import pallas as pl
from jax.experimental.pallas import tpu as pltpu
from jax.sharding import PartitionSpec as P

SEG_LEN = 4096
LAGS = 256
DOPLEN = 512
DOPK = 256
OFFS = 4
WINDOW = 512
LANES = 128
GROUP = 4
SHARE = 4
UNITS = SEG_LEN // LANES
BLOCKS = SEG_LEN // 256
LAG_DEV = 32
HALF_ROWS = SHARE
SPLIT = 2
CHUNKS = SHARE * SPLIT
LAG_STEPS = 2
CHUNK = UNITS // SPLIT
VMEM_LIMIT = 67043328 - 10800 * 1024

MESH = pl.DeviceIdType.MESH

PAIRS = (
    ((0, 5), (1, 4)),
    ((0, 0), (1, 5), (2, 4)),
    ((0, 1), (1, 0), (2, 5), (3, 4)),
    ((0, 2), (1, 1), (2, 0), (3, 5)),
    ((2, 1), (3, 0)),
    ((3, 1),),
)


def split_table(table):
    table = table.astype(np.float32)
    high = table.astype(ml_dtypes.bfloat16)
    low = (table - high.astype(np.float32)).astype(ml_dtypes.bfloat16)
    return np.stack([high, low])


def forward_table():
    sample = np.arange(WINDOW)[:, None]
    freq = np.arange(WINDOW // 2)[None, :] + 0.5
    angle = 2.0 * np.pi / WINDOW * sample * freq
    return split_table(np.concatenate([np.cos(angle), np.sin(angle)], axis=1))


def inverse_table():
    lag = np.arange(LAGS)[None, :]
    freq = np.arange(WINDOW // 2)[:, None] + 0.5
    angle = 2.0 * np.pi / WINDOW * lag * freq
    return split_table(np.concatenate([np.cos(angle), np.sin(angle)], axis=0) / WINDOW)


def doppler_table(parts):
    seg = np.arange(parts * GROUP * SHARE).reshape(parts, GROUP, SHARE, 1)
    freq = np.arange(DOPK) - DOPK // 2
    angle = 2.0 * np.pi / DOPLEN * (seg * freq % DOPLEN)
    cos, sin = np.cos(angle), -np.sin(angle)
    real_rows = np.concatenate([cos, sin], axis=-1)
    imag_rows = np.concatenate([-sin, cos], axis=-1)
    table = np.stack([real_rows, imag_rows], axis=3)
    return split_table(table.reshape(parts * GROUP * 2 * SHARE, 2 * DOPK))


def halves(value):
    high = value.astype(jnp.bfloat16)
    low = (value - high.astype(jnp.float32)).astype(jnp.bfloat16)
    return high, low


def product(value, high_table, low_table):
    rows = value.shape[0]
    high, low = halves(value)
    both = jnp.dot(
        jnp.concatenate([high, low], axis=0), high_table, preferred_element_type=jnp.float32
    )
    small = jnp.dot(high, low_table, preferred_element_type=jnp.float32)
    return both[:rows] + (both[rows:] + small)


def store_spectra(mixed, ref, side, start):
    rows, half = mixed.shape[0] // 2, mixed.shape[1] // 2
    a_cos, a_sin = mixed[:rows, :half], mixed[:rows, half:]
    b_cos, b_sin = mixed[rows:, :half], mixed[rows:, half:]
    parts = (a_cos + b_sin, b_cos - a_sin, a_cos - b_sin, b_cos + a_sin)
    for index, part in enumerate(parts):
        ref[side, start : start + rows, index * half : (index + 1) * half] = part


def row_sums(values):
    index = lax.broadcasted_iota(jnp.int32, values[0].shape, 0)
    step = 1
    while len(values) > 1:
        first = index // step % 2 == 0
        values = [
            jnp.where(first, a, b) + pltpu.roll(jnp.where(first, b, a), step, 0)
            for a, b in zip(values[0::2], values[1::2])
        ]
        step *= 2
    return values[0]


def kernel(
    planes,
    parts,
    x_ref,
    fwd_hbm,
    inv_hbm,
    dop_hbm,
    out_ref,
    buf,
    qs,
    ps,
    srow,
    corr,
    ct,
    fin,
    low,
    fwd,
    inv,
    dop,
    table_sem,
    send_plane,
    send_z,
    recv_x,
    send_c,
    recv_c,
    ready,
):
    rx, tm = lax.axis_index("rx"), lax.axis_index("tm")
    count = planes * GROUP
    me = rx % GROUP
    base = rx - me
    below = (base + count - GROUP) % count
    above = (base + GROUP) % count

    def other(k):
        return (me // 2 + k // 2) % 2 * 2 + (me % 2 + k % 2) % 2

    def part_of_x(index, chunk):
        start = pl.multiple_of((index * CHUNKS + chunk) * CHUNK, CHUNK)
        return x_ref.at[:, pl.ds(start, CHUNK), :]

    def place(slot, chunk):
        start = pl.multiple_of(chunk % SPLIT * CHUNK, CHUNK)
        return buf.at[slot, chunk // SPLIT, :, pl.ds(start, CHUNK), :]

    def own_copy(seg):
        start = pl.multiple_of((me * SHARE + seg) * UNITS, UNITS)
        return pltpu.make_async_copy(
            x_ref.at[:, pl.ds(start, UNITS), :], buf.at[me, seg], recv_x.at[me, seg]
        )

    def plane_copy(k, chunk):
        j = other(k)
        return pltpu.make_async_remote_copy(
            src_ref=part_of_x(j, chunk),
            dst_ref=place(me, chunk),
            send_sem=send_plane.at[k - 1, chunk],
            recv_sem=recv_x.at[me, chunk],
            device_id=(base + j, tm),
            device_id_type=MESH,
        )

    def z_copy(k, chunk, src):
        j = other(k)
        return pltpu.make_async_remote_copy(
            src_ref=src,
            dst_ref=place(GROUP + j, chunk),
            send_sem=send_z.at[k, chunk],
            recv_sem=recv_x.at[GROUP + j, chunk],
            device_id=((rx + count + (j // 2 * 2 - 1) * GROUP) % count, tm),
            device_id_type=MESH,
        )

    def received(ref, sem):
        return pltpu.make_async_remote_copy(
            src_ref=ref,
            dst_ref=ref,
            send_sem=send_c.at[0, 0],
            recv_sem=sem,
            device_id=(rx, tm),
            device_id_type=MESH,
        )

    tables = [
        pltpu.make_async_copy(fwd_hbm, fwd, table_sem.at[0]),
        pltpu.make_async_copy(inv_hbm, inv, table_sem.at[1]),
        pltpu.make_async_copy(dop_hbm, dop, table_sem.at[2]),
    ]

    barrier = pltpu.get_barrier_semaphore()

    def greet(r, t):
        pl.semaphore_signal(barrier, 1, device_id=(r, t), device_id_type=MESH)

    greet(below + me, tm)
    greet(above + me, tm)
    for k in range(1, GROUP):
        greet(base + other(k), tm)
    for step in range(1, parts):
        greet(rx, (tm + step) % parts)
    for copy in tables:
        copy.start()
    for seg in range(SHARE):
        own_copy(seg).start()
    pl.semaphore_wait(barrier, 2 + GROUP - 1 + parts - 1)

    for chunk in range(CHUNKS):
        for k in (3, 2, 1):
            plane_copy(k, chunk).start()
        z_copy(0, chunk, part_of_x(me, chunk)).start()

    for k in range(1, GROUP):
        pl.semaphore_signal(ready.at[0], 1, device_id=(base + other(k), tm), device_id_type=MESH)
    pl.semaphore_signal(ready.at[1], 1, device_id=(above + me, tm), device_id_type=MESH)
    tables[0].wait()
    pl.semaphore_wait(ready.at[1], 1)

    @pl.when(me < 2)
    def _():
        for k in range(GROUP):
            to = below + other(k)
            pl.semaphore_signal(ready.at[2], 1, device_id=(to, tm), device_id_type=MESH)

    def pieces(slot, seg, comp):
        rows = buf.at[slot, seg, comp]
        even = rows[pl.ds(0, BLOCKS, stride=2), :]
        odd = rows[pl.ds(1, BLOCKS, stride=2), :]
        return even, odd

    def window(slot, seg, comp):
        even, odd = pieces(slot, seg, comp)
        before = pltpu.roll(odd, 1, 0)
        after = pltpu.roll(even, BLOCKS - 1, 0)
        return jnp.concatenate([before, even, odd, after], axis=1)

    def window_spectra(slots, seg, side):
        rows = [window(slot, seg, comp) for comp in range(2) for slot in slots]
        mixed = product(jnp.concatenate(rows, axis=0), fwd[0], fwd[1])
        store_spectra(mixed, qs, side, slots[0] * BLOCKS)

    def block_spectra(slots, seg, side, target):
        rows = [
            jnp.concatenate(pieces(slot, seg, comp), axis=1) for comp in range(2) for slot in slots
        ]
        mixed = product(
            jnp.concatenate(rows, axis=0), fwd[0, : WINDOW // 2], fwd[1, : WINDOW // 2]
        )
        store_spectra(mixed, ps, side, target * BLOCKS)

    order = [(slot, off, far) for slot, partners in enumerate(PAIRS) for off, far in partners]

    def correlate(seg, side):
        def half_step(half, carry):
            def part(ref, slot, index):
                start = pl.multiple_of(index * (WINDOW // 2) + half * LANES, LANES)
                return ref[side, slot * BLOCKS : (slot + 1) * BLOCKS, pl.ds(start, LANES)]

            for group in range(2):
                sums = []
                for slot, _, far in order[group * 8 : group * 8 + 8]:
                    q = [part(qs, slot, i) for i in range(4)]
                    p = [part(ps, far, i) for i in range(4)]
                    z = [
                        q[0] * p[0] + q[1] * p[1],
                        q[1] * p[0] - q[0] * p[1],
                        q[2] * p[2] + q[3] * p[3],
                        q[3] * p[2] - q[2] * p[3],
                    ]
                    z = [v[:8] + v[8:] for v in z]
                    sums.append([z[0] + z[2], z[3] - z[1], z[1] + z[3], z[0] - z[2]])
                for i in range(4):
                    row = pl.multiple_of(seg * 32 + i // 2 * 16 + group * 8, 8)
                    lane = pl.multiple_of(i % 2 * (WINDOW // 2) + half * LANES, LANES)
                    srow[pl.ds(row, 8), pl.ds(lane, LANES)] = row_sums([v[i] for v in sums])
            return carry

        lax.fori_loop(0, 2, half_step, 0)

    def arrived(slot, chunk):
        received(place(slot, chunk), recv_x.at[slot, chunk]).wait_recv()

    def seg_step(step, carry):
        @pl.when(step < SHARE)
        def _():
            for part in range(SPLIT):
                chunk = step * SPLIT + part
                for k in range(1, GROUP):
                    arrived(other(k), chunk)
                    z_copy(k, chunk, place(other(k), chunk)).start()
            own_copy(step).wait()
            window_spectra(range(0, 4), step, step)
            block_spectra(range(0, 3), step, step, 0)

        @pl.when(step >= LAG_STEPS)
        def _():
            seg = step - LAG_STEPS
            for part in range(SPLIT):
                for slot in range(GROUP, 2 * GROUP):
                    arrived(slot, seg * SPLIT + part)
            window_spectra(range(4, 6), seg, seg)
            block_spectra(range(6, 8), seg, seg, 4)
            correlate(seg, seg)

        return carry

    lane = lax.broadcasted_iota(jnp.int32, (HALF_ROWS, LANES), 1)

    def tile_copy(k, step, half):
        j, to = other(k), (tm + step) % parts
        rows = pl.ds(half * HALF_ROWS, HALF_ROWS)
        return pltpu.make_async_remote_copy(
            src_ref=ct.at[j, to, rows],
            dst_ref=fin.at[tm, me, rows],
            send_sem=send_c.at[half, min(k, 1)],
            recv_sem=recv_c.at[half, min(k, 1)],
            device_id=(base + j, to),
            device_id_type=MESH,
        )

    def low_copy(i, step, half):
        to = (tm + step) % parts
        rows = pl.ds(half * HALF_ROWS, HALF_ROWS)
        return pltpu.make_async_remote_copy(
            src_ref=ct.at[GROUP + i, to, rows],
            dst_ref=low.at[tm, me, rows],
            send_sem=send_c.at[half, 2],
            recv_sem=recv_c.at[half, 2],
            device_id=(above + i, to),
            device_id_type=MESH,
        )

    def tiles(slots, half):
        first = half * SHARE * 16
        for slot in slots:
            for col in range(2):
                values = [
                    (off, corr[col, pl.ds(first + index, HALF_ROWS, stride=16), :])
                    for index, (at, off, _) in enumerate(order)
                    if at == slot
                ]
                for piece in range(4):
                    if col * 4 + piece >= parts:
                        continue
                    tile = jnp.zeros((HALF_ROWS, LANES), jnp.float32)
                    for off, value in values:
                        shift = LAG_DEV * (off - piece) % LANES
                        if shift:
                            value = pltpu.roll(value, shift, 1)
                        tile = jnp.where(lane // LAG_DEV == off, value, tile)
                    rows = slice(half * HALF_ROWS, (half + 1) * HALF_ROWS)
                    ct[slot, col * 4 + piece, rows] = tile

    steps = sorted(range(parts), key=lambda step: -min(step % 4, -step % 4))

    def send_lags(half):
        rows = slice(half * SHARE * 16, (half + 1) * SHARE * 16)
        lags = product(srow[rows], inv[0], inv[1])
        corr[0, rows], corr[1, rows] = lags[:, :LANES], lags[:, LANES:]
        tiles((4, 5), half)
        for step in steps:
            for i in range(2):
                low_copy(i, step, half).start()
        tiles(range(4), half)
        for ks in ((3, 2), (1, 0)):
            for step in steps:
                for k in ks:
                    if k or step:
                        tile_copy(k, step, half).start()

    lax.fori_loop(0, SHARE // 2 + LAG_STEPS, seg_step, 0)
    tables[1].wait()
    pl.semaphore_wait(ready.at[0], GROUP - 1)
    pl.semaphore_wait(ready.at[2], 2)
    send_lags(0)
    lax.fori_loop(SHARE // 2 + LAG_STEPS, SHARE + LAG_STEPS, seg_step, 0)
    send_lags(1)

    fin[tm, me] = ct[me, tm]
    tables[2].wait()
    for chunk in range(CHUNKS):
        for k in range(GROUP):
            if k:
                plane_copy(k, chunk).wait_send()
            z_copy(k, chunk, part_of_x(me, chunk)).wait_send()

    for half in range(2):
        rows = pl.ds(half * HALF_ROWS, HALF_ROWS)

        @pl.when(me < 2)
        def _():
            received(low.at[:, :, rows], recv_c.at[half, 2]).wait_recv()

        received(fin.at[:, : GROUP - 1, rows], recv_c.at[half, 1]).wait_recv()
        received(fin.at[: parts - 1, 0, rows], recv_c.at[half, 0]).wait_recv()

    rows = parts * GROUP * 2 * SHARE
    lanes = lax.broadcasted_iota(jnp.int32, (rows, LANES), 1)
    columns = jnp.where(
        lanes < 2 * LAG_DEV + LAG_DEV * me,
        fin[...].reshape(rows, LANES),
        low[...].reshape(rows, LANES),
    )
    result = product(columns.T, dop[0], dop[1])
    for off in range(OFFS):
        for col in range(4):
            out_ref[pl.ds(col // 2 * 8 + off * 2 + col % 2, LAG_DEV, stride=16), :] = result[
                off * LAG_DEV : (off + 1) * LAG_DEV, col * LANES : (col + 1) * LANES
            ]

    def sent(ref, sem):
        pltpu.make_async_remote_copy(
            src_ref=ref,
            dst_ref=ref,
            send_sem=sem,
            recv_sem=recv_c.at[0, 0],
            device_id=(rx, tm),
            device_id_type=MESH,
        ).wait_send()

    for half in range(2):
        rows = pl.ds(half * HALF_ROWS, HALF_ROWS)
        sent(ct.at[0, : parts - 1, rows], send_c.at[half, 0])
        sent(ct.at[: GROUP - 1, :, rows], send_c.at[half, 1])
        sent(ct.at[GROUP : GROUP + 2, :, rows], send_c.at[half, 2])


def per_device(planes, parts, signals):
    rows = signals.reshape(2, -1, LANES)
    dop_rows = parts * GROUP * 2 * SHARE
    dma, vmem = pltpu.SemaphoreType.DMA, pltpu.VMEM
    out = pl.pallas_call(
        functools.partial(kernel, planes, parts),
        out_shape=jax.ShapeDtypeStruct((LAG_DEV * 2 * OFFS * 2, LANES), jnp.float32),
        in_specs=[pl.BlockSpec(memory_space=pl.ANY)] * 4,
        out_specs=pl.BlockSpec(memory_space=pltpu.VMEM),
        scratch_shapes=[
            vmem((2 * GROUP, SHARE, 2, UNITS, LANES), jnp.float32),
            vmem((SHARE, 6 * BLOCKS, 2 * WINDOW), jnp.float32),
            vmem((SHARE, 6 * BLOCKS, 2 * WINDOW), jnp.float32),
            vmem((SHARE * 32, WINDOW), jnp.float32),
            vmem((2, SHARE * 32, LANES), jnp.float32),
            vmem((6, parts, 8, LANES), jnp.float32),
            vmem((parts, GROUP, 8, LANES), jnp.float32),
            vmem((parts, GROUP, 8, LANES), jnp.float32),
            vmem((2, WINDOW, WINDOW), jnp.bfloat16),
            vmem((2, WINDOW, LAGS), jnp.bfloat16),
            vmem((2, dop_rows, 2 * DOPK), jnp.bfloat16),
            dma((3,)),
            dma((GROUP - 1, CHUNKS)),
            dma((GROUP, CHUNKS)),
            dma((2 * GROUP, CHUNKS)),
            dma((2, 3)),
            dma((2, 3)),
            pltpu.SemaphoreType.REGULAR((3,)),
        ],
        compiler_params=pltpu.CompilerParams(
            collective_id=0, has_side_effects=True, vmem_limit_bytes=VMEM_LIMIT
        ),
        name="ambiguity",
    )(
        rows,
        jnp.asarray(forward_table()),
        jnp.asarray(inverse_table()),
        jnp.asarray(doppler_table(parts)),
    )
    scale = 1.0 / math.sqrt(2.0 * SEG_LEN * parts * GROUP * SHARE)
    return out.reshape(LAG_DEV, 2, 1, OFFS, 1, DOPK) * jnp.float32(scale)


def solution(mesh):
    planes, parts = mesh.shape["rx"] // GROUP, mesh.shape["tm"]
    return jax.shard_map(
        functools.partial(per_device, planes, parts),
        mesh=mesh,
        in_specs=(P(None, "rx", "tm"),),
        out_specs=P("tm", None, "rx", None, None, None),
        check_vma=False,
    )
```

```python
import functools
import math

import jax
import jax.numpy as jnp
import ml_dtypes
import numpy as np
from jax import lax
from jax.experimental import pallas as pl
from jax.experimental.pallas import tpu as pltpu
from jax.sharding import PartitionSpec as P

SEG_LEN = 4096
LAGS = 256
DOPLEN = 512
DOPK = 256
OFFS = 4
WINDOW = 512
LANES = 128
GROUP = 4
SHARE = 4
UNITS = SEG_LEN // LANES
BLOCKS = SEG_LEN // 256
LAG_DEV = 32
HALF_ROWS = SHARE
SPLIT = 1
CHUNKS = SHARE * SPLIT
LAG_STEPS = 3
CHUNK = UNITS // SPLIT
VMEM_LIMIT = 67043328 - 10800 * 1024

MESH = pl.DeviceIdType.MESH

PAIRS = (
    ((0, 5), (1, 4)),
    ((0, 0), (1, 5), (2, 4)),
    ((0, 1), (1, 0), (2, 5), (3, 4)),
    ((0, 2), (1, 1), (2, 0), (3, 5)),
    ((2, 1), (3, 0)),
    ((3, 1),),
)


def split_table(table):
    table = table.astype(np.float32)
    high = table.astype(ml_dtypes.bfloat16)
    low = (table - high.astype(np.float32)).astype(ml_dtypes.bfloat16)
    return np.stack([high, low])


def forward_table():
    sample = np.arange(WINDOW)[:, None]
    freq = np.arange(WINDOW // 2)[None, :] + 0.5
    angle = 2.0 * np.pi / WINDOW * sample * freq
    return split_table(np.concatenate([np.cos(angle), np.sin(angle)], axis=1))


def inverse_table():
    lag = np.arange(LAGS)[None, :]
    freq = np.arange(WINDOW // 2)[:, None] + 0.5
    angle = 2.0 * np.pi / WINDOW * lag * freq
    return split_table(np.concatenate([np.cos(angle), np.sin(angle)], axis=0) / WINDOW)


def doppler_table(parts):
    seg = np.arange(parts * GROUP * SHARE).reshape(parts, GROUP, SHARE, 1)
    freq = np.arange(DOPK) - DOPK // 2
    angle = 2.0 * np.pi / DOPLEN * (seg * freq % DOPLEN)
    cos, sin = np.cos(angle), -np.sin(angle)
    real_rows = np.concatenate([cos, sin], axis=-1)
    imag_rows = np.concatenate([-sin, cos], axis=-1)
    table = np.stack([real_rows, imag_rows], axis=3)
    return split_table(table.reshape(parts * GROUP * 2 * SHARE, 2 * DOPK))


def halves(value):
    high = value.astype(jnp.bfloat16)
    low = (value - high.astype(jnp.float32)).astype(jnp.bfloat16)
    return high, low


def product(value, high_table, low_table):
    rows = value.shape[0]
    high, low = halves(value)
    both = jnp.dot(
        jnp.concatenate([high, low], axis=0), high_table, preferred_element_type=jnp.float32
    )
    small = jnp.dot(high, low_table, preferred_element_type=jnp.float32)
    return both[:rows] + (both[rows:] + small)


def store_spectra(mixed, ref, side, start):
    rows, half = mixed.shape[0] // 2, mixed.shape[1] // 2
    a_cos, a_sin = mixed[:rows, :half], mixed[:rows, half:]
    b_cos, b_sin = mixed[rows:, :half], mixed[rows:, half:]
    parts = (a_cos + b_sin, b_cos - a_sin, a_cos - b_sin, b_cos + a_sin)
    for index, part in enumerate(parts):
        ref[side, start : start + rows, index * half : (index + 1) * half] = part


def row_sums(values):
    index = lax.broadcasted_iota(jnp.int32, values[0].shape, 0)
    step = 1
    while len(values) > 1:
        first = index // step % 2 == 0
        values = [
            jnp.where(first, a, b) + pltpu.roll(jnp.where(first, b, a), step, 0)
            for a, b in zip(values[0::2], values[1::2])
        ]
        step *= 2
    return values[0]


def kernel(
    planes,
    parts,
    x_ref,
    fwd_hbm,
    inv_hbm,
    dop_hbm,
    out_ref,
    buf,
    qs,
    ps,
    srow,
    corr,
    ct,
    fin,
    low,
    fwd,
    inv,
    dop,
    table_sem,
    own_sem,
    send_x,
    recv_plane,
    recv_z,
    send_c,
    recv_c,
    ready,
):
    rx, tm = lax.axis_index("rx"), lax.axis_index("tm")
    count = planes * GROUP
    me = rx % GROUP
    base = rx - me
    below = (base + count - GROUP) % count
    above = (base + GROUP) % count

    def other(k):
        return (me // 2 + k // 2) % 2 * 2 + (me % 2 + k % 2) % 2

    def part_of_x(index, chunk):
        start = pl.multiple_of((index * CHUNKS + chunk) * CHUNK, CHUNK)
        return x_ref.at[:, pl.ds(start, CHUNK), :]

    def place(slot, chunk):
        return buf.at[slot, :, pl.ds(pl.multiple_of(chunk * CHUNK, CHUNK), CHUNK), :]

    own = pltpu.make_async_copy(
        x_ref.at[:, pl.ds(pl.multiple_of(me * SHARE * UNITS, UNITS), SHARE * UNITS), :],
        buf.at[me],
        own_sem,
    )

    def plane_copy(k, chunk):
        j = other(k)
        return pltpu.make_async_remote_copy(
            src_ref=part_of_x(j, chunk),
            dst_ref=place(me, chunk),
            send_sem=send_x.at[0],
            recv_sem=recv_plane.at[chunk],
            device_id=(base + j, tm),
            device_id_type=MESH,
        )

    def z_copy(k, chunk, src):
        j = other(k)
        return pltpu.make_async_remote_copy(
            src_ref=src,
            dst_ref=place(GROUP + j, chunk),
            send_sem=send_x.at[1],
            recv_sem=recv_z.at[chunk],
            device_id=((rx + count + (j // 2 * 2 - 1) * GROUP) % count, tm),
            device_id_type=MESH,
        )

    def received(ref, sem):
        return pltpu.make_async_remote_copy(
            src_ref=ref,
            dst_ref=ref,
            send_sem=send_c,
            recv_sem=sem,
            device_id=(rx, tm),
            device_id_type=MESH,
        )

    tables = [
        pltpu.make_async_copy(fwd_hbm, fwd, table_sem.at[0]),
        pltpu.make_async_copy(inv_hbm, inv, table_sem.at[1]),
        pltpu.make_async_copy(dop_hbm, dop, table_sem.at[2]),
    ]

    barrier = pltpu.get_barrier_semaphore()

    def greet(r, t):
        pl.semaphore_signal(barrier, 1, device_id=(r, t), device_id_type=MESH)

    greet(below + me, tm)
    greet(above + me, tm)
    for k in range(1, GROUP):
        greet(base + other(k), tm)
    for step in range(1, parts):
        greet(rx, (tm + step) % parts)
    for copy in tables:
        copy.start()
    own.start()
    pl.semaphore_wait(barrier, 2 + GROUP - 1 + parts - 1)

    for chunk in range(CHUNKS):
        for k in (3, 2, 1):
            plane_copy(k, chunk).start()
        z_copy(0, chunk, part_of_x(me, chunk)).start()

    for k in range(1, GROUP):
        pl.semaphore_signal(ready.at[0], 1, device_id=(base + other(k), tm), device_id_type=MESH)
    pl.semaphore_signal(ready.at[1], 1, device_id=(above + me, tm), device_id_type=MESH)
    tables[0].wait()
    pl.semaphore_wait(ready.at[1], 1)

    @pl.when(me < 2)
    def _():
        for k in range(GROUP):
            to = below + other(k)
            pl.semaphore_signal(ready.at[2], 1, device_id=(to, tm), device_id_type=MESH)

    def pieces(slot, seg, comp):
        rows = buf.at[slot, comp, pl.ds(pl.multiple_of(seg * UNITS, UNITS), UNITS), :]
        even = rows[pl.ds(0, BLOCKS, stride=2), :]
        odd = rows[pl.ds(1, BLOCKS, stride=2), :]
        return even, odd

    def window(slot, seg, comp):
        even, odd = pieces(slot, seg, comp)
        before = pltpu.roll(odd, 1, 0)
        after = pltpu.roll(even, BLOCKS - 1, 0)
        return jnp.concatenate([before, even, odd, after], axis=1)

    def window_spectra(slots, seg, side):
        rows = [window(slot, seg, comp) for comp in range(2) for slot in slots]
        mixed = product(jnp.concatenate(rows, axis=0), fwd[0], fwd[1])
        store_spectra(mixed, qs, side, slots[0] * BLOCKS)

    def block_spectra(slots, seg, side, target):
        rows = [
            jnp.concatenate(pieces(slot, seg, comp), axis=1) for comp in range(2) for slot in slots
        ]
        mixed = product(
            jnp.concatenate(rows, axis=0), fwd[0, : WINDOW // 2], fwd[1, : WINDOW // 2]
        )
        store_spectra(mixed, ps, side, target * BLOCKS)

    order = [(slot, off, far) for slot, partners in enumerate(PAIRS) for off, far in partners]

    def correlate(seg, side):
        def half_step(half, carry):
            def part(ref, slot, index):
                start = pl.multiple_of(index * (WINDOW // 2) + half * LANES, LANES)
                return ref[side, slot * BLOCKS : (slot + 1) * BLOCKS, pl.ds(start, LANES)]

            for group in range(2):
                sums = []
                for slot, _, far in order[group * 8 : group * 8 + 8]:
                    q = [part(qs, slot, i) for i in range(4)]
                    p = [part(ps, far, i) for i in range(4)]
                    z = [
                        q[0] * p[0] + q[1] * p[1],
                        q[1] * p[0] - q[0] * p[1],
                        q[2] * p[2] + q[3] * p[3],
                        q[3] * p[2] - q[2] * p[3],
                    ]
                    z = [v[:8] + v[8:] for v in z]
                    sums.append([z[0] + z[2], z[3] - z[1], z[1] + z[3], z[0] - z[2]])
                for i in range(4):
                    row = pl.multiple_of(seg * 32 + i // 2 * 16 + group * 8, 8)
                    lane = pl.multiple_of(i % 2 * (WINDOW // 2) + half * LANES, LANES)
                    srow[pl.ds(row, 8), pl.ds(lane, LANES)] = row_sums([v[i] for v in sums])
            return carry

        lax.fori_loop(0, 2, half_step, 0)

    def arrived(slots, chunk, sem):
        received(place(slots, chunk), sem.at[chunk]).wait_recv()

    def seg_step(step, carry):
        @pl.when(step < SHARE)
        def _():
            for part in range(SPLIT):
                chunk = step * SPLIT + part
                arrived(slice(0, GROUP - 1), chunk, recv_plane)
                for k in (2, 3, 1):
                    z_copy(k, chunk, place(other(k), chunk)).start()

            @pl.when(step == 0)
            def _():
                own.wait()

            window_spectra(range(0, 4), step, step)
            block_spectra(range(0, 3), step, step, 0)

        @pl.when(step >= LAG_STEPS)
        def _():
            seg = step - LAG_STEPS
            for part in range(SPLIT):
                arrived(slice(GROUP, 2 * GROUP), seg * SPLIT + part, recv_z)
            window_spectra(range(4, 6), seg, seg)
            block_spectra(range(6, 8), seg, seg, 4)
            correlate(seg, seg)

        return carry

    lane = lax.broadcasted_iota(jnp.int32, (HALF_ROWS, LANES), 1)

    def tile_copy(k, step, half):
        j, to = other(k), (tm + step) % parts
        rows = pl.ds(half * HALF_ROWS, HALF_ROWS)
        return pltpu.make_async_remote_copy(
            src_ref=ct.at[j * parts + to, rows],
            dst_ref=fin.at[tm * GROUP + me, rows],
            send_sem=send_c,
            recv_sem=recv_c.at[0],
            device_id=(base + j, to),
            device_id_type=MESH,
        )

    def low_copy(i, step, half):
        to = (tm + step) % parts
        rows = pl.ds(half * HALF_ROWS, HALF_ROWS)
        return pltpu.make_async_remote_copy(
            src_ref=ct.at[(GROUP + i) * parts + to, rows],
            dst_ref=low.at[tm * GROUP + me, rows],
            send_sem=send_c,
            recv_sem=recv_c.at[1],
            device_id=(above + i, to),
            device_id_type=MESH,
        )

    def tiles(slots, half):
        first = half * SHARE * 16
        for slot in slots:
            for col in range(2):
                values = [
                    (off, corr[col, pl.ds(first + index, HALF_ROWS, stride=16), :])
                    for index, (at, off, _) in enumerate(order)
                    if at == slot
                ]
                for piece in range(4):
                    if col * 4 + piece >= parts:
                        continue
                    tile = jnp.zeros((HALF_ROWS, LANES), jnp.float32)
                    for off, value in values:
                        shift = LAG_DEV * (off - piece) % LANES
                        if shift:
                            value = pltpu.roll(value, shift, 1)
                        tile = jnp.where(lane // LAG_DEV == off, value, tile)
                    rows = slice(half * HALF_ROWS, (half + 1) * HALF_ROWS)
                    ct[slot * parts + col * 4 + piece, rows] = tile

    steps = sorted(range(parts), key=lambda step: -min(step % 4, -step % 4))

    def send_lags(half):
        rows = slice(half * SHARE * 16, (half + 1) * SHARE * 16)
        lags = product(srow[rows], inv[0], inv[1])
        corr[0, rows], corr[1, rows] = lags[:, :LANES], lags[:, LANES:]
        tiles((4, 5), half)
        for step in steps:
            for i in range(2):
                low_copy(i, step, half).start()
        tiles(range(4), half)
        for ks in ((3, 2), (1, 0)):
            for step in steps:
                for k in ks:
                    if k or step:
                        tile_copy(k, step, half).start()

    lax.fori_loop(0, SHARE // 2 + LAG_STEPS, seg_step, 0)
    tables[1].wait()
    pl.semaphore_wait(ready.at[0], GROUP - 1)
    pl.semaphore_wait(ready.at[2], 2)
    send_lags(0)
    lax.fori_loop(SHARE // 2 + LAG_STEPS, SHARE + LAG_STEPS, seg_step, 0)
    send_lags(1)

    fin[tm * GROUP + me] = ct[me * parts + tm]
    tables[2].wait()

    def sent(ref, sem):
        pltpu.make_async_remote_copy(
            src_ref=ref,
            dst_ref=ref,
            send_sem=sem,
            recv_sem=recv_c.at[0],
            device_id=(rx, tm),
            device_id_type=MESH,
        ).wait_send()

    sent(buf.at[: GROUP - 1], send_x.at[0])
    sent(buf.at[:GROUP], send_x.at[1])

    @pl.when(me < 2)
    def _():
        received(low, recv_c.at[1]).wait_recv()

    received(fin.at[: parts * GROUP - 1], recv_c.at[0]).wait_recv()

    rows = parts * GROUP * 2 * SHARE
    lanes = lax.broadcasted_iota(jnp.int32, (rows, LANES), 1)
    columns = jnp.where(
        lanes < 2 * LAG_DEV + LAG_DEV * me,
        fin[...].reshape(rows, LANES),
        low[...].reshape(rows, LANES),
    )
    result = product(columns.T, dop[0], dop[1])
    for off in range(OFFS):
        for col in range(4):
            out_ref[pl.ds(col // 2 * 8 + off * 2 + col % 2, LAG_DEV, stride=16), :] = result[
                off * LAG_DEV : (off + 1) * LAG_DEV, col * LANES : (col + 1) * LANES
            ]

    sent(ct.at[: 6 * parts - 1], send_c)


def per_device(planes, parts, signals):
    rows = signals.reshape(2, -1, LANES)
    dop_rows = parts * GROUP * 2 * SHARE
    dma, vmem = pltpu.SemaphoreType.DMA, pltpu.VMEM
    out = pl.pallas_call(
        functools.partial(kernel, planes, parts),
        out_shape=jax.ShapeDtypeStruct((LAG_DEV * 2 * OFFS * 2, LANES), jnp.float32),
        in_specs=[pl.BlockSpec(memory_space=pl.ANY)] * 4,
        out_specs=pl.BlockSpec(memory_space=pltpu.VMEM),
        scratch_shapes=[
            vmem((2 * GROUP, 2, SHARE * UNITS, LANES), jnp.float32),
            vmem((SHARE, 6 * BLOCKS, 2 * WINDOW), jnp.float32),
            vmem((SHARE, 6 * BLOCKS, 2 * WINDOW), jnp.float32),
            vmem((SHARE * 32, WINDOW), jnp.float32),
            vmem((2, SHARE * 32, LANES), jnp.float32),
            vmem((6 * parts, 8, LANES), jnp.float32),
            vmem((parts * GROUP, 8, LANES), jnp.float32),
            vmem((parts * GROUP, 8, LANES), jnp.float32),
            vmem((2, WINDOW, WINDOW), jnp.bfloat16),
            vmem((2, WINDOW, LAGS), jnp.bfloat16),
            vmem((2, dop_rows, 2 * DOPK), jnp.bfloat16),
            dma((3,)),
            dma,
            dma((2,)),
            dma((CHUNKS,)),
            dma((CHUNKS,)),
            dma,
            dma((2,)),
            pltpu.SemaphoreType.REGULAR((3,)),
        ],
        compiler_params=pltpu.CompilerParams(
            collective_id=0, has_side_effects=True, vmem_limit_bytes=VMEM_LIMIT
        ),
        name="ambiguity",
    )(
        rows,
        jnp.asarray(forward_table()),
        jnp.asarray(inverse_table()),
        jnp.asarray(doppler_table(parts)),
    )
    scale = 1.0 / math.sqrt(2.0 * SEG_LEN * parts * GROUP * SHARE)
    return out.reshape(LAG_DEV, 2, 1, OFFS, 1, DOPK) * jnp.float32(scale)


def solution(mesh):
    planes, parts = mesh.shape["rx"] // GROUP, mesh.shape["tm"]
    return jax.shard_map(
        functools.partial(per_device, planes, parts),
        mesh=mesh,
        in_specs=(P(None, "rx", "tm"),),
        out_specs=P("tm", None, "rx", None, None, None),
        check_vma=False,
    )
```

```python
import functools
import math

import jax
import jax.numpy as jnp
import ml_dtypes
import numpy as np
from jax import lax
from jax.experimental import pallas as pl
from jax.experimental.pallas import tpu as pltpu
from jax.sharding import PartitionSpec as P

SEG_LEN = 4096
LAGS = 256
DOPLEN = 512
DOPK = 256
OFFS = 4
WINDOW = 512
LANES = 128
GROUP = 4
SHARE = 4
UNITS = SEG_LEN // LANES
BLOCKS = SEG_LEN // 256
LAG_DEV = 32
HALF_ROWS = SHARE
SPLIT = 2
CHUNKS = SHARE * SPLIT
LAG_STEPS = 3
CHUNK = UNITS // SPLIT
VMEM_LIMIT = 67043328 - 10800 * 1024

MESH = pl.DeviceIdType.MESH

PAIRS = (
    ((0, 5), (1, 4)),
    ((0, 0), (1, 5), (2, 4)),
    ((0, 1), (1, 0), (2, 5), (3, 4)),
    ((0, 2), (1, 1), (2, 0), (3, 5)),
    ((2, 1), (3, 0)),
    ((3, 1),),
)


def split_table(table):
    table = table.astype(np.float32)
    high = table.astype(ml_dtypes.bfloat16)
    low = (table - high.astype(np.float32)).astype(ml_dtypes.bfloat16)
    return np.stack([high, low])


def forward_table():
    sample = np.arange(WINDOW)[:, None]
    freq = np.arange(WINDOW // 2)[None, :] + 0.5
    angle = 2.0 * np.pi / WINDOW * sample * freq
    return split_table(np.concatenate([np.cos(angle), np.sin(angle)], axis=1))


def inverse_table():
    lag = np.arange(LAGS)[None, :]
    freq = np.arange(WINDOW // 2)[:, None] + 0.5
    angle = 2.0 * np.pi / WINDOW * lag * freq
    return split_table(np.concatenate([np.cos(angle), np.sin(angle)], axis=0) / WINDOW)


def doppler_table(parts):
    seg = np.arange(parts * GROUP * SHARE).reshape(parts, GROUP, SHARE, 1)
    freq = np.arange(DOPK) - DOPK // 2
    angle = 2.0 * np.pi / DOPLEN * (seg * freq % DOPLEN)
    cos, sin = np.cos(angle), -np.sin(angle)
    real_rows = np.concatenate([cos, sin], axis=-1)
    imag_rows = np.concatenate([-sin, cos], axis=-1)
    table = np.stack([real_rows, imag_rows], axis=3)
    return split_table(table.reshape(parts * GROUP * 2 * SHARE, 2 * DOPK))


def halves(value):
    high = value.astype(jnp.bfloat16)
    low = (value - high.astype(jnp.float32)).astype(jnp.bfloat16)
    return high, low


def product(value, high_table, low_table):
    rows = value.shape[0]
    high, low = halves(value)
    both = jnp.dot(
        jnp.concatenate([high, low], axis=0), high_table, preferred_element_type=jnp.float32
    )
    small = jnp.dot(high, low_table, preferred_element_type=jnp.float32)
    return both[:rows] + (both[rows:] + small)


def store_spectra(mixed, ref, side, start):
    rows, half = mixed.shape[0] // 2, mixed.shape[1] // 2
    a_cos, a_sin = mixed[:rows, :half], mixed[:rows, half:]
    b_cos, b_sin = mixed[rows:, :half], mixed[rows:, half:]
    parts = (a_cos + b_sin, b_cos - a_sin, a_cos - b_sin, b_cos + a_sin)
    for index, part in enumerate(parts):
        ref[side, start : start + rows, index * half : (index + 1) * half] = part


def row_sums(values):
    index = lax.broadcasted_iota(jnp.int32, (8, LANES), 0)
    zero = jnp.zeros((8, LANES), jnp.float32)
    step = 1
    while len(values) > 1:
        first = index // step % 2 == 0
        pairs = list(zip(values[0::2], values[1::2]))
        values = []
        for a, b in pairs:
            if a is None and b is None:
                values.append(None)
                continue
            a, b = zero if a is None else a, zero if b is None else b
            values.append(jnp.where(first, a, b) + pltpu.roll(jnp.where(first, b, a), step, 0))
        step *= 2
    return values[0]


def kernel(
    planes,
    parts,
    x_ref,
    fwd_hbm,
    inv_hbm,
    dop_hbm,
    out_ref,
    buf,
    qs,
    ps,
    srow,
    corr,
    ct,
    fin,
    low,
    fwd,
    inv,
    dop,
    table_sem,
    own_sem,
    send_x,
    recv_plane,
    recv_z,
    send_c,
    recv_c,
    ready,
):
    rx, tm = lax.axis_index("rx"), lax.axis_index("tm")
    count = planes * GROUP
    me = rx % GROUP
    base = rx - me
    below = (base + count - GROUP) % count
    above = (base + GROUP) % count

    def other(k):
        return (me // 2 + k // 2) % 2 * 2 + (me % 2 + k % 2) % 2

    def part_of_x(index, chunk):
        start = pl.multiple_of((index * CHUNKS + chunk) * CHUNK, CHUNK)
        return x_ref.at[:, pl.ds(start, CHUNK), :]

    def place(slot, chunk):
        return buf.at[slot, :, pl.ds(pl.multiple_of(chunk * CHUNK, CHUNK), CHUNK), :]

    own = pltpu.make_async_copy(
        x_ref.at[:, pl.ds(pl.multiple_of(me * SHARE * UNITS, UNITS), SHARE * UNITS), :],
        buf.at[me],
        own_sem,
    )

    def plane_copy(k, chunk):
        j = other(k)
        return pltpu.make_async_remote_copy(
            src_ref=part_of_x(j, chunk),
            dst_ref=place(me, chunk),
            send_sem=send_x.at[0],
            recv_sem=recv_plane.at[chunk],
            device_id=(base + j, tm),
            device_id_type=MESH,
        )

    def z_copy(k, chunk, src):
        j = other(k)
        return pltpu.make_async_remote_copy(
            src_ref=src,
            dst_ref=place(GROUP + j, chunk),
            send_sem=send_x.at[1],
            recv_sem=recv_z.at[chunk],
            device_id=((rx + count + (j // 2 * 2 - 1) * GROUP) % count, tm),
            device_id_type=MESH,
        )

    def received(ref, sem):
        return pltpu.make_async_remote_copy(
            src_ref=ref,
            dst_ref=ref,
            send_sem=send_c,
            recv_sem=sem,
            device_id=(rx, tm),
            device_id_type=MESH,
        )

    tables = [
        pltpu.make_async_copy(fwd_hbm, fwd, table_sem.at[0]),
        pltpu.make_async_copy(inv_hbm, inv, table_sem.at[1]),
        pltpu.make_async_copy(dop_hbm, dop, table_sem.at[2]),
    ]

    barrier = pltpu.get_barrier_semaphore()

    def greet(r, t):
        pl.semaphore_signal(barrier, 1, device_id=(r, t), device_id_type=MESH)

    greet(below + me, tm)
    greet(above + me, tm)
    for k in range(1, GROUP):
        greet(base + other(k), tm)
    for step in range(1, parts):
        greet(rx, (tm + step) % parts)
    for copy in tables:
        copy.start()
    own.start()
    pl.semaphore_wait(barrier, 2 + GROUP - 1 + parts - 1)

    for chunk in range(CHUNKS):
        for k in (3, 2, 1):
            plane_copy(k, chunk).start()
        z_copy(0, chunk, part_of_x(me, chunk)).start()

    for k in range(1, GROUP):
        pl.semaphore_signal(ready.at[0], 1, device_id=(base + other(k), tm), device_id_type=MESH)
    pl.semaphore_signal(ready.at[1], 1, device_id=(above + me, tm), device_id_type=MESH)
    tables[0].wait()
    pl.semaphore_wait(ready.at[1], 1)

    @pl.when(me < 2)
    def _():
        for k in range(GROUP):
            to = below + other(k)
            pl.semaphore_signal(ready.at[2], 1, device_id=(to, tm), device_id_type=MESH)

    def pieces(slot, seg, comp):
        rows = buf.at[slot, comp, pl.ds(pl.multiple_of(seg * UNITS, UNITS), UNITS), :]
        even = rows[pl.ds(0, BLOCKS, stride=2), :]
        odd = rows[pl.ds(1, BLOCKS, stride=2), :]
        return even, odd

    def window(slot, seg, comp):
        even, odd = pieces(slot, seg, comp)
        before = pltpu.roll(odd, 1, 0)
        after = pltpu.roll(even, BLOCKS - 1, 0)
        return jnp.concatenate([before, even, odd, after], axis=1)

    def window_spectra(slots, seg, side):
        rows = [window(slot, seg, comp) for comp in range(2) for slot in slots]
        mixed = product(jnp.concatenate(rows, axis=0), fwd[0], fwd[1])
        store_spectra(mixed, qs, side, slots[0] * BLOCKS)

    def block_spectra(slots, seg, side, target):
        rows = [
            jnp.concatenate(pieces(slot, seg, comp), axis=1) for comp in range(2) for slot in slots
        ]
        mixed = product(
            jnp.concatenate(rows, axis=0), fwd[0, : WINDOW // 2], fwd[1, : WINDOW // 2]
        )
        store_spectra(mixed, ps, side, target * BLOCKS)

    order = [(slot, off, far) for slot, partners in enumerate(PAIRS) for off, far in partners]
    order.sort(key=lambda entry: entry[0] >= GROUP or entry[2] >= GROUP - 1)
    inner = sum(slot < GROUP and far < GROUP - 1 for slot, _, far in order)

    def correlate(seg, first, last):
        def half_step(half, carry):
            def part(ref, slot, index):
                start = pl.multiple_of(index * (WINDOW // 2) + half * LANES, LANES)
                return ref[seg, slot * BLOCKS : (slot + 1) * BLOCKS, pl.ds(start, LANES)]

            for group in range(2):
                places = range(group * 8, group * 8 + 8)
                if not any(first <= place < last for place in places):
                    continue
                sums = []
                for place in places:
                    if not first <= place < last:
                        sums.append([None] * 4)
                        continue
                    slot, _, far = order[place]
                    q = [part(qs, slot, i) for i in range(4)]
                    p = [part(ps, far, i) for i in range(4)]
                    z = [
                        q[0] * p[0] + q[1] * p[1],
                        q[1] * p[0] - q[0] * p[1],
                        q[2] * p[2] + q[3] * p[3],
                        q[3] * p[2] - q[2] * p[3],
                    ]
                    z = [v[:8] + v[8:] for v in z]
                    sums.append([z[0] + z[2], z[3] - z[1], z[1] + z[3], z[0] - z[2]])
                for i in range(4):
                    row = pl.multiple_of(seg * 32 + i // 2 * 16 + group * 8, 8)
                    lane = pl.multiple_of(i % 2 * (WINDOW // 2) + half * LANES, LANES)
                    total = row_sums([v[i] for v in sums])
                    if places[0] < first:
                        total += srow[pl.ds(row, 8), pl.ds(lane, LANES)]
                    srow[pl.ds(row, 8), pl.ds(lane, LANES)] = total
            return carry

        lax.fori_loop(0, 2, half_step, 0)

    def arrived(slots, chunk, sem):
        received(place(slots, chunk), sem.at[chunk]).wait_recv()

    def seg_step(step, carry):
        @pl.when(step < SHARE)
        def _():
            for part in range(SPLIT):
                chunk = step * SPLIT + part
                arrived(slice(0, GROUP - 1), chunk, recv_plane)
                for k in (2, 3, 1):
                    z_copy(k, chunk, place(other(k), chunk)).start()

            @pl.when(step == 0)
            def _():
                own.wait()

            window_spectra(range(0, 4), step, step)
            block_spectra(range(0, 3), step, step, 0)
            correlate(step, 0, inner)

        @pl.when(step >= LAG_STEPS)
        def _():
            seg = step - LAG_STEPS
            for part in range(SPLIT):
                arrived(slice(GROUP, 2 * GROUP), seg * SPLIT + part, recv_z)
            window_spectra(range(4, 6), seg, seg)
            block_spectra(range(6, 8), seg, seg, 4)
            correlate(seg, inner, len(order))

        return carry

    lane = lax.broadcasted_iota(jnp.int32, (HALF_ROWS, LANES), 1)

    def tile_copy(k, step, half):
        j, to = other(k), (tm + step) % parts
        rows = pl.ds(half * HALF_ROWS, HALF_ROWS)
        return pltpu.make_async_remote_copy(
            src_ref=ct.at[j * parts + to, rows],
            dst_ref=fin.at[tm * GROUP + me, rows],
            send_sem=send_c,
            recv_sem=recv_c.at[0],
            device_id=(base + j, to),
            device_id_type=MESH,
        )

    def low_copy(i, step, half):
        to = (tm + step) % parts
        rows = pl.ds(half * HALF_ROWS, HALF_ROWS)
        return pltpu.make_async_remote_copy(
            src_ref=ct.at[(GROUP + i) * parts + to, rows],
            dst_ref=low.at[tm * GROUP + me, rows],
            send_sem=send_c,
            recv_sem=recv_c.at[1],
            device_id=(above + i, to),
            device_id_type=MESH,
        )

    def tiles(slots, half):
        first = half * SHARE * 16
        for slot in slots:
            for col in range(2):
                values = [
                    (off, corr[col, pl.ds(first + index, HALF_ROWS, stride=16), :])
                    for index, (at, off, _) in enumerate(order)
                    if at == slot
                ]
                for piece in range(4):
                    if col * 4 + piece >= parts:
                        continue
                    tile = jnp.zeros((HALF_ROWS, LANES), jnp.float32)
                    for off, value in values:
                        shift = LAG_DEV * (off - piece) % LANES
                        if shift:
                            value = pltpu.roll(value, shift, 1)
                        tile = jnp.where(lane // LAG_DEV == off, value, tile)
                    rows = slice(half * HALF_ROWS, (half + 1) * HALF_ROWS)
                    ct[slot * parts + col * 4 + piece, rows] = tile

    steps = sorted(range(parts), key=lambda step: -min(step % 4, -step % 4))

    def send_lags(half):
        rows = slice(half * SHARE * 16, (half + 1) * SHARE * 16)
        lags = product(srow[rows], inv[0], inv[1])
        corr[0, rows], corr[1, rows] = lags[:, :LANES], lags[:, LANES:]
        tiles((4, 5), half)
        for step in steps:
            for i in range(2):
                low_copy(i, step, half).start()
        tiles(range(4), half)
        for ks in ((3, 2), (1, 0)):
            for step in steps:
                for k in ks:
                    if k or step:
                        tile_copy(k, step, half).start()

    lax.fori_loop(0, SHARE // 2 + LAG_STEPS, seg_step, 0)
    tables[1].wait()
    pl.semaphore_wait(ready.at[0], GROUP - 1)
    pl.semaphore_wait(ready.at[2], 2)
    send_lags(0)
    lax.fori_loop(SHARE // 2 + LAG_STEPS, SHARE + LAG_STEPS, seg_step, 0)
    send_lags(1)

    fin[tm * GROUP + me] = ct[me * parts + tm]
    tables[2].wait()

    def sent(ref, sem):
        pltpu.make_async_remote_copy(
            src_ref=ref,
            dst_ref=ref,
            send_sem=sem,
            recv_sem=recv_c.at[0],
            device_id=(rx, tm),
            device_id_type=MESH,
        ).wait_send()

    sent(buf.at[: GROUP - 1], send_x.at[0])
    sent(buf.at[:GROUP], send_x.at[1])

    @pl.when(me < 2)
    def _():
        received(low, recv_c.at[1]).wait_recv()

    received(fin.at[: parts * GROUP - 1], recv_c.at[0]).wait_recv()

    rows = parts * GROUP * 2 * SHARE
    lanes = lax.broadcasted_iota(jnp.int32, (rows, LANES), 1)
    columns = jnp.where(
        lanes < 2 * LAG_DEV + LAG_DEV * me,
        fin[...].reshape(rows, LANES),
        low[...].reshape(rows, LANES),
    )
    result = product(columns.T, dop[0], dop[1])
    for off in range(OFFS):
        for col in range(4):
            out_ref[pl.ds(col // 2 * 8 + off * 2 + col % 2, LAG_DEV, stride=16), :] = result[
                off * LAG_DEV : (off + 1) * LAG_DEV, col * LANES : (col + 1) * LANES
            ]

    sent(ct.at[: 6 * parts - 1], send_c)


def per_device(planes, parts, signals):
    rows = signals.reshape(2, -1, LANES)
    dop_rows = parts * GROUP * 2 * SHARE
    dma, vmem = pltpu.SemaphoreType.DMA, pltpu.VMEM
    out = pl.pallas_call(
        functools.partial(kernel, planes, parts),
        out_shape=jax.ShapeDtypeStruct((LAG_DEV * 2 * OFFS * 2, LANES), jnp.float32),
        in_specs=[pl.BlockSpec(memory_space=pl.ANY)] * 4,
        out_specs=pl.BlockSpec(memory_space=pltpu.VMEM),
        scratch_shapes=[
            vmem((2 * GROUP, 2, SHARE * UNITS, LANES), jnp.float32),
            vmem((SHARE, 6 * BLOCKS, 2 * WINDOW), jnp.float32),
            vmem((SHARE, 6 * BLOCKS, 2 * WINDOW), jnp.float32),
            vmem((SHARE * 32, WINDOW), jnp.float32),
            vmem((2, SHARE * 32, LANES), jnp.float32),
            vmem((6 * parts, 8, LANES), jnp.float32),
            vmem((parts * GROUP, 8, LANES), jnp.float32),
            vmem((parts * GROUP, 8, LANES), jnp.float32),
            vmem((2, WINDOW, WINDOW), jnp.bfloat16),
            vmem((2, WINDOW, LAGS), jnp.bfloat16),
            vmem((2, dop_rows, 2 * DOPK), jnp.bfloat16),
            dma((3,)),
            dma,
            dma((2,)),
            dma((CHUNKS,)),
            dma((CHUNKS,)),
            dma,
            dma((2,)),
            pltpu.SemaphoreType.REGULAR((3,)),
        ],
        compiler_params=pltpu.CompilerParams(
            collective_id=0, has_side_effects=True, vmem_limit_bytes=VMEM_LIMIT
        ),
        name="ambiguity",
    )(
        rows,
        jnp.asarray(forward_table()),
        jnp.asarray(inverse_table()),
        jnp.asarray(doppler_table(parts)),
    )
    scale = 1.0 / math.sqrt(2.0 * SEG_LEN * parts * GROUP * SHARE)
    return out.reshape(LAG_DEV, 2, 1, OFFS, 1, DOPK) * jnp.float32(scale)


def solution(mesh):
    planes, parts = mesh.shape["rx"] // GROUP, mesh.shape["tm"]
    return jax.shard_map(
        functools.partial(per_device, planes, parts),
        mesh=mesh,
        in_specs=(P(None, "rx", "tm"),),
        out_specs=P("tm", None, "rx", None, None, None),
        check_vma=False,
    )
```

```python
import functools
import math

import jax
import jax.numpy as jnp
import ml_dtypes
import numpy as np
from jax import lax
from jax.experimental import pallas as pl
from jax.experimental.pallas import tpu as pltpu
from jax.sharding import PartitionSpec as P

SEG_LEN = 4096
LAGS = 256
DOPLEN = 512
DOPK = 256
OFFS = 4
WINDOW = 512
LANES = 128
GROUP = 4
SHARE = 4
UNITS = SEG_LEN // LANES
BLOCKS = SEG_LEN // 256
LAG_DEV = 32
HALF_ROWS = SHARE
SPLIT = 2
CHUNKS = SHARE * SPLIT
LAG_STEPS = 4
CHUNK = UNITS // SPLIT
VMEM_LIMIT = 67043328 - 10800 * 1024

MESH = pl.DeviceIdType.MESH

PAIRS = (
    ((0, 5), (1, 4)),
    ((0, 0), (1, 5), (2, 4)),
    ((0, 1), (1, 0), (2, 5), (3, 4)),
    ((0, 2), (1, 1), (2, 0), (3, 5)),
    ((2, 1), (3, 0)),
    ((3, 1),),
)


def split_table(table):
    table = table.astype(np.float32)
    high = table.astype(ml_dtypes.bfloat16)
    low = (table - high.astype(np.float32)).astype(ml_dtypes.bfloat16)
    return np.stack([high, low])


def forward_table():
    sample = np.arange(WINDOW)[:, None]
    freq = np.arange(WINDOW // 2)[None, :] + 0.5
    angle = 2.0 * np.pi / WINDOW * sample * freq
    return split_table(np.concatenate([np.cos(angle), np.sin(angle)], axis=1))


def inverse_table():
    lag = np.arange(LAGS)[None, :]
    freq = np.arange(WINDOW // 2)[:, None] + 0.5
    angle = 2.0 * np.pi / WINDOW * lag * freq
    return split_table(np.concatenate([np.cos(angle), np.sin(angle)], axis=0) / WINDOW)


def doppler_table(parts):
    seg = np.arange(parts * GROUP * SHARE).reshape(parts, GROUP, SHARE, 1)
    freq = np.arange(DOPK) - DOPK // 2
    angle = 2.0 * np.pi / DOPLEN * (seg * freq % DOPLEN)
    cos, sin = np.cos(angle), -np.sin(angle)
    real_rows = np.concatenate([cos, sin], axis=-1)
    imag_rows = np.concatenate([-sin, cos], axis=-1)
    table = np.stack([real_rows, imag_rows], axis=3)
    return split_table(table.reshape(parts * GROUP * 2 * SHARE, 2 * DOPK))


def halves(value):
    high = value.astype(jnp.bfloat16)
    low = (value - high.astype(jnp.float32)).astype(jnp.bfloat16)
    return high, low


def product(value, high_table, low_table):
    rows = value.shape[0]
    high, low = halves(value)
    both = jnp.dot(
        jnp.concatenate([high, low], axis=0), high_table, preferred_element_type=jnp.float32
    )
    small = jnp.dot(high, low_table, preferred_element_type=jnp.float32)
    return both[:rows] + (both[rows:] + small)


def store_spectra(mixed, ref, side, start):
    rows, half = mixed.shape[0] // 2, mixed.shape[1] // 2
    a_cos, a_sin = mixed[:rows, :half], mixed[:rows, half:]
    b_cos, b_sin = mixed[rows:, :half], mixed[rows:, half:]
    parts = (a_cos + b_sin, b_cos - a_sin, a_cos - b_sin, b_cos + a_sin)
    for index, part in enumerate(parts):
        ref[side, start : start + rows, index * half : (index + 1) * half] = part


def row_sums(values):
    index = lax.broadcasted_iota(jnp.int32, (8, LANES), 0)
    zero = jnp.zeros((8, LANES), jnp.float32)
    step = 1
    while len(values) > 1:
        first = index // step % 2 == 0
        pairs = list(zip(values[0::2], values[1::2]))
        values = []
        for a, b in pairs:
            if a is None and b is None:
                values.append(None)
                continue
            a, b = zero if a is None else a, zero if b is None else b
            values.append(jnp.where(first, a, b) + pltpu.roll(jnp.where(first, b, a), step, 0))
        step *= 2
    return values[0]


def kernel(
    planes,
    parts,
    x_ref,
    fwd_hbm,
    inv_hbm,
    dop_hbm,
    out_ref,
    buf,
    qs,
    ps,
    srow,
    corr,
    ct,
    fin,
    low,
    fwd,
    inv,
    dop,
    table_sem,
    own_sem,
    send_x,
    recv_plane,
    recv_z,
    send_c,
    recv_c,
    ready,
):
    rx, tm = lax.axis_index("rx"), lax.axis_index("tm")
    count = planes * GROUP
    me = rx % GROUP
    base = rx - me
    below = (base + count - GROUP) % count
    above = (base + GROUP) % count

    def other(k):
        return (me // 2 + k // 2) % 2 * 2 + (me % 2 + k % 2) % 2

    def part_of_x(index, chunk):
        start = pl.multiple_of((index * CHUNKS + chunk) * CHUNK, CHUNK)
        return x_ref.at[:, pl.ds(start, CHUNK), :]

    def place(slot, chunk):
        return buf.at[slot, :, pl.ds(pl.multiple_of(chunk * CHUNK, CHUNK), CHUNK), :]

    own = pltpu.make_async_copy(
        x_ref.at[:, pl.ds(pl.multiple_of(me * SHARE * UNITS, UNITS), SHARE * UNITS), :],
        buf.at[me],
        own_sem,
    )

    def plane_copy(k, chunk):
        j = other(k)
        return pltpu.make_async_remote_copy(
            src_ref=part_of_x(j, chunk),
            dst_ref=place(me, chunk),
            send_sem=send_x.at[0],
            recv_sem=recv_plane.at[chunk],
            device_id=(base + j, tm),
            device_id_type=MESH,
        )

    def z_copy(k, chunk, src):
        j = other(k)
        return pltpu.make_async_remote_copy(
            src_ref=src,
            dst_ref=place(GROUP + j, chunk),
            send_sem=send_x.at[1],
            recv_sem=recv_z.at[chunk],
            device_id=((rx + count + (j // 2 * 2 - 1) * GROUP) % count, tm),
            device_id_type=MESH,
        )

    def received(ref, sem):
        return pltpu.make_async_remote_copy(
            src_ref=ref,
            dst_ref=ref,
            send_sem=send_c,
            recv_sem=sem,
            device_id=(rx, tm),
            device_id_type=MESH,
        )

    tables = [
        pltpu.make_async_copy(fwd_hbm, fwd, table_sem.at[0]),
        pltpu.make_async_copy(inv_hbm, inv, table_sem.at[1]),
        pltpu.make_async_copy(dop_hbm, dop, table_sem.at[2]),
    ]

    barrier = pltpu.get_barrier_semaphore()

    def greet(r, t):
        pl.semaphore_signal(barrier, 1, device_id=(r, t), device_id_type=MESH)

    greet(below + me, tm)
    greet(above + me, tm)
    for k in range(1, GROUP):
        greet(base + other(k), tm)
    for step in range(1, parts):
        greet(rx, (tm + step) % parts)
    for copy in tables:
        copy.start()
    own.start()
    pl.semaphore_wait(barrier, 2 + GROUP - 1 + parts - 1)

    for chunk in range(CHUNKS):
        for k in (3, 2, 1) if chunk % 2 else (2, 3, 1):
            plane_copy(k, chunk).start()
        z_copy(0, chunk, part_of_x(me, chunk)).start()

    for k in range(1, GROUP):
        pl.semaphore_signal(ready.at[0], 1, device_id=(base + other(k), tm), device_id_type=MESH)
    pl.semaphore_signal(ready.at[1], 1, device_id=(above + me, tm), device_id_type=MESH)
    tables[0].wait()
    pl.semaphore_wait(ready.at[1], 1)

    @pl.when(me < 2)
    def _():
        for k in range(GROUP):
            to = below + other(k)
            pl.semaphore_signal(ready.at[2], 1, device_id=(to, tm), device_id_type=MESH)

    def pieces(slot, seg, comp):
        rows = buf.at[slot, comp, pl.ds(pl.multiple_of(seg * UNITS, UNITS), UNITS), :]
        even = rows[pl.ds(0, BLOCKS, stride=2), :]
        odd = rows[pl.ds(1, BLOCKS, stride=2), :]
        return even, odd

    def window(slot, seg, comp):
        even, odd = pieces(slot, seg, comp)
        before = pltpu.roll(odd, 1, 0)
        after = pltpu.roll(even, BLOCKS - 1, 0)
        return jnp.concatenate([before, even, odd, after], axis=1)

    def window_spectra(slots, seg, side):
        rows = [window(slot, seg, comp) for comp in range(2) for slot in slots]
        mixed = product(jnp.concatenate(rows, axis=0), fwd[0], fwd[1])
        store_spectra(mixed, qs, side, slots[0] * BLOCKS)

    def block_spectra(slots, seg, side, target):
        rows = [
            jnp.concatenate(pieces(slot, seg, comp), axis=1) for comp in range(2) for slot in slots
        ]
        mixed = product(
            jnp.concatenate(rows, axis=0), fwd[0, : WINDOW // 2], fwd[1, : WINDOW // 2]
        )
        store_spectra(mixed, ps, side, target * BLOCKS)

    order = [(slot, off, far) for slot, partners in enumerate(PAIRS) for off, far in partners]
    order.sort(key=lambda entry: entry[0] >= GROUP or entry[2] >= GROUP - 1)
    inner = sum(slot < GROUP and far < GROUP - 1 for slot, _, far in order)

    def correlate(seg, first, last):
        def half_step(half, carry):
            def part(ref, slot, index):
                start = pl.multiple_of(index * (WINDOW // 2) + half * LANES, LANES)
                return ref[seg, slot * BLOCKS : (slot + 1) * BLOCKS, pl.ds(start, LANES)]

            for group in range(2):
                places = range(group * 8, group * 8 + 8)
                if not any(first <= place < last for place in places):
                    continue
                sums = []
                for place in places:
                    if not first <= place < last:
                        sums.append([None] * 4)
                        continue
                    slot, _, far = order[place]
                    q = [part(qs, slot, i) for i in range(4)]
                    p = [part(ps, far, i) for i in range(4)]
                    z = [
                        q[0] * p[0] + q[1] * p[1],
                        q[1] * p[0] - q[0] * p[1],
                        q[2] * p[2] + q[3] * p[3],
                        q[3] * p[2] - q[2] * p[3],
                    ]
                    z = [v[:8] + v[8:] for v in z]
                    sums.append([z[0] + z[2], z[3] - z[1], z[1] + z[3], z[0] - z[2]])
                for i in range(4):
                    row = pl.multiple_of(seg * 32 + i // 2 * 16 + group * 8, 8)
                    lane = pl.multiple_of(i % 2 * (WINDOW // 2) + half * LANES, LANES)
                    total = row_sums([v[i] for v in sums])
                    if places[0] < first:
                        total += srow[pl.ds(row, 8), pl.ds(lane, LANES)]
                    srow[pl.ds(row, 8), pl.ds(lane, LANES)] = total
            return carry

        lax.fori_loop(0, 2, half_step, 0)

    def arrived(slots, chunk, sem):
        received(place(slots, chunk), sem.at[chunk]).wait_recv()

    def seg_step(step, carry):
        @pl.when(step < SHARE)
        def _():
            for part in range(SPLIT):
                chunk = step * SPLIT + part
                arrived(slice(0, GROUP - 1), chunk, recv_plane)
                for k in (2, 3, 1):
                    z_copy(k, chunk, place(other(k), chunk)).start()

            @pl.when(step == 0)
            def _():
                own.wait()

            window_spectra(range(0, 4), step, step)
            block_spectra(range(0, 3), step, step, 0)
            correlate(step, 0, inner)

        @pl.when(step >= LAG_STEPS)
        def _():
            seg = step - LAG_STEPS
            for part in range(SPLIT):
                arrived(slice(GROUP, 2 * GROUP), seg * SPLIT + part, recv_z)
            window_spectra(range(4, 6), seg, seg)
            block_spectra(range(6, 8), seg, seg, 4)
            correlate(seg, inner, len(order))

        return carry

    lane = lax.broadcasted_iota(jnp.int32, (HALF_ROWS, LANES), 1)

    def tile_copy(k, step, half):
        j, to = other(k), (tm + step) % parts
        rows = pl.ds(half * HALF_ROWS, HALF_ROWS)
        return pltpu.make_async_remote_copy(
            src_ref=ct.at[j * parts + to, rows],
            dst_ref=fin.at[tm * GROUP + me, rows],
            send_sem=send_c,
            recv_sem=recv_c.at[0],
            device_id=(base + j, to),
            device_id_type=MESH,
        )

    def low_copy(i, step, half):
        to = (tm + step) % parts
        rows = pl.ds(half * HALF_ROWS, HALF_ROWS)
        return pltpu.make_async_remote_copy(
            src_ref=ct.at[(GROUP + i) * parts + to, rows],
            dst_ref=low.at[tm * GROUP + me, rows],
            send_sem=send_c,
            recv_sem=recv_c.at[1],
            device_id=(above + i, to),
            device_id_type=MESH,
        )

    def tiles(slots, half):
        first = half * SHARE * 16
        for slot in slots:
            for col in range(2):
                values = [
                    (off, corr[col, pl.ds(first + index, HALF_ROWS, stride=16), :])
                    for index, (at, off, _) in enumerate(order)
                    if at == slot
                ]
                for piece in range(4):
                    if col * 4 + piece >= parts:
                        continue
                    tile = jnp.zeros((HALF_ROWS, LANES), jnp.float32)
                    for off, value in values:
                        shift = LAG_DEV * (off - piece) % LANES
                        if shift:
                            value = pltpu.roll(value, shift, 1)
                        tile = jnp.where(lane // LAG_DEV == off, value, tile)
                    rows = slice(half * HALF_ROWS, (half + 1) * HALF_ROWS)
                    ct[slot * parts + col * 4 + piece, rows] = tile

    steps = sorted(range(parts), key=lambda step: -min(step % 4, -step % 4))

    def send_lags(half):
        rows = slice(half * SHARE * 16, (half + 1) * SHARE * 16)
        lags = product(srow[rows], inv[0], inv[1])
        corr[0, rows], corr[1, rows] = lags[:, :LANES], lags[:, LANES:]
        tiles(range(6), half)
        for step in steps:
            for i in range(2):
                low_copy(i, step, half).start()
        for ks in ((3, 2), (1, 0)):
            for step in steps:
                for k in ks:
                    if k or step:
                        tile_copy(k, step, half).start()

    lax.fori_loop(0, SHARE // 2 + LAG_STEPS, seg_step, 0)
    tables[1].wait()
    pl.semaphore_wait(ready.at[0], GROUP - 1)
    pl.semaphore_wait(ready.at[2], 2)
    send_lags(0)
    lax.fori_loop(SHARE // 2 + LAG_STEPS, SHARE + LAG_STEPS, seg_step, 0)
    send_lags(1)

    fin[tm * GROUP + me] = ct[me * parts + tm]
    tables[2].wait()

    def sent(ref, sem):
        pltpu.make_async_remote_copy(
            src_ref=ref,
            dst_ref=ref,
            send_sem=sem,
            recv_sem=recv_c.at[0],
            device_id=(rx, tm),
            device_id_type=MESH,
        ).wait_send()

    sent(buf.at[: GROUP - 1], send_x.at[0])
    sent(buf.at[:GROUP], send_x.at[1])

    @pl.when(me < 2)
    def _():
        received(low, recv_c.at[1]).wait_recv()

    received(fin.at[: parts * GROUP - 1], recv_c.at[0]).wait_recv()

    rows = parts * GROUP * 2 * SHARE
    lanes = lax.broadcasted_iota(jnp.int32, (rows, LANES), 1)
    columns = jnp.where(
        lanes < 2 * LAG_DEV + LAG_DEV * me,
        fin[...].reshape(rows, LANES),
        low[...].reshape(rows, LANES),
    )
    result = product(columns.T, dop[0], dop[1])
    for off in range(OFFS):
        for col in range(4):
            out_ref[pl.ds(col // 2 * 8 + off * 2 + col % 2, LAG_DEV, stride=16), :] = result[
                off * LAG_DEV : (off + 1) * LAG_DEV, col * LANES : (col + 1) * LANES
            ]

    sent(ct.at[: 6 * parts - 1], send_c)


def per_device(planes, parts, signals):
    rows = signals.reshape(2, -1, LANES)
    dop_rows = parts * GROUP * 2 * SHARE
    dma, vmem = pltpu.SemaphoreType.DMA, pltpu.VMEM
    out = pl.pallas_call(
        functools.partial(kernel, planes, parts),
        out_shape=jax.ShapeDtypeStruct((LAG_DEV * 2 * OFFS * 2, LANES), jnp.float32),
        in_specs=[pl.BlockSpec(memory_space=pl.ANY)] * 4,
        out_specs=pl.BlockSpec(memory_space=pltpu.VMEM),
        scratch_shapes=[
            vmem((2 * GROUP, 2, SHARE * UNITS, LANES), jnp.float32),
            vmem((SHARE, 6 * BLOCKS, 2 * WINDOW), jnp.float32),
            vmem((SHARE, 6 * BLOCKS, 2 * WINDOW), jnp.float32),
            vmem((SHARE * 32, WINDOW), jnp.float32),
            vmem((2, SHARE * 32, LANES), jnp.float32),
            vmem((6 * parts, 8, LANES), jnp.float32),
            vmem((parts * GROUP, 8, LANES), jnp.float32),
            vmem((parts * GROUP, 8, LANES), jnp.float32),
            vmem((2, WINDOW, WINDOW), jnp.bfloat16),
            vmem((2, WINDOW, LAGS), jnp.bfloat16),
            vmem((2, dop_rows, 2 * DOPK), jnp.bfloat16),
            dma((3,)),
            dma,
            dma((2,)),
            dma((CHUNKS,)),
            dma((CHUNKS,)),
            dma,
            dma((2,)),
            pltpu.SemaphoreType.REGULAR((3,)),
        ],
        compiler_params=pltpu.CompilerParams(
            collective_id=0, has_side_effects=True, vmem_limit_bytes=VMEM_LIMIT
        ),
        name="ambiguity",
    )(
        rows,
        jnp.asarray(forward_table()),
        jnp.asarray(inverse_table()),
        jnp.asarray(doppler_table(parts)),
    )
    scale = 1.0 / math.sqrt(2.0 * SEG_LEN * parts * GROUP * SHARE)
    return out.reshape(LAG_DEV, 2, 1, OFFS, 1, DOPK) * jnp.float32(scale)


def solution(mesh):
    planes, parts = mesh.shape["rx"] // GROUP, mesh.shape["tm"]
    return jax.shard_map(
        functools.partial(per_device, planes, parts),
        mesh=mesh,
        in_specs=(P(None, "rx", "tm"),),
        out_specs=P("tm", None, "rx", None, None, None),
        check_vma=False,
    )
```

```python
import functools
import math

import jax
import jax.numpy as jnp
import ml_dtypes
import numpy as np
from jax import lax
from jax.experimental import pallas as pl
from jax.experimental.pallas import tpu as pltpu
from jax.sharding import PartitionSpec as P

SEG_LEN = 4096
LAGS = 256
DOPLEN = 512
DOPK = 256
OFFS = 4
WINDOW = 512
LANES = 128
GROUP = 4
SHARE = 4
UNITS = SEG_LEN // LANES
BLOCKS = SEG_LEN // 256
LAG_DEV = 32
HALF_ROWS = SHARE
SPLIT = 2
CHUNKS = SHARE * SPLIT
LAG_STEPS = 3
CHUNK = UNITS // SPLIT
VMEM_LIMIT = 67043328 - 10800 * 1024

MESH = pl.DeviceIdType.MESH

PAIRS = (
    ((0, 5), (1, 4)),
    ((0, 0), (1, 5), (2, 4)),
    ((0, 1), (1, 0), (2, 5), (3, 4)),
    ((0, 2), (1, 1), (2, 0), (3, 5)),
    ((2, 1), (3, 0)),
    ((3, 1),),
)


def split_table(table):
    table = table.astype(np.float32)
    high = table.astype(ml_dtypes.bfloat16)
    low = (table - high.astype(np.float32)).astype(ml_dtypes.bfloat16)
    return np.stack([high, low])


def forward_table():
    sample = np.arange(WINDOW)[:, None]
    freq = np.arange(WINDOW // 2)[None, :] + 0.5
    angle = 2.0 * np.pi / WINDOW * sample * freq
    return split_table(np.concatenate([np.cos(angle), np.sin(angle)], axis=1))


def inverse_table():
    lag = np.arange(LAGS)[None, :]
    freq = np.arange(WINDOW // 2)[:, None] + 0.5
    angle = 2.0 * np.pi / WINDOW * lag * freq
    return split_table(np.concatenate([np.cos(angle), np.sin(angle)], axis=0) / WINDOW)


def doppler_table(parts):
    seg = np.arange(parts * GROUP * SHARE).reshape(parts, GROUP, SHARE, 1)
    freq = np.arange(DOPK) - DOPK // 2
    angle = 2.0 * np.pi / DOPLEN * (seg * freq % DOPLEN)
    cos, sin = np.cos(angle), -np.sin(angle)
    real_rows = np.concatenate([cos, sin], axis=-1)
    imag_rows = np.concatenate([-sin, cos], axis=-1)
    table = np.stack([real_rows, imag_rows], axis=3)
    return split_table(table.reshape(parts * GROUP * 2 * SHARE, 2 * DOPK))


def halves(value):
    high = value.astype(jnp.bfloat16)
    low = (value - high.astype(jnp.float32)).astype(jnp.bfloat16)
    return high, low


def product(value, high_table, low_table):
    rows = value.shape[0]
    high, low = halves(value)
    both = jnp.dot(
        jnp.concatenate([high, low], axis=0), high_table, preferred_element_type=jnp.float32
    )
    small = jnp.dot(high, low_table, preferred_element_type=jnp.float32)
    return both[:rows] + (both[rows:] + small)


def store_spectra(mixed, ref, side, start):
    rows, half = mixed.shape[0] // 2, mixed.shape[1] // 2
    a_cos, a_sin = mixed[:rows, :half], mixed[:rows, half:]
    b_cos, b_sin = mixed[rows:, :half], mixed[rows:, half:]
    parts = (a_cos + b_sin, b_cos - a_sin, a_cos - b_sin, b_cos + a_sin)
    for index, part in enumerate(parts):
        ref[side, start : start + rows, index * half : (index + 1) * half] = part


def row_sums(values):
    index = lax.broadcasted_iota(jnp.int32, (8, LANES), 0)
    zero = jnp.zeros((8, LANES), jnp.float32)
    step = 1
    while len(values) > 1:
        first = index // step % 2 == 0
        pairs = list(zip(values[0::2], values[1::2]))
        values = []
        for a, b in pairs:
            if a is None and b is None:
                values.append(None)
                continue
            a, b = zero if a is None else a, zero if b is None else b
            values.append(jnp.where(first, a, b) + pltpu.roll(jnp.where(first, b, a), step, 0))
        step *= 2
    return values[0]


def kernel(
    planes,
    parts,
    x_ref,
    fwd_hbm,
    inv_hbm,
    dop_hbm,
    out_ref,
    buf,
    qs,
    ps,
    srow,
    corr,
    ct,
    fin,
    low,
    fwd,
    inv,
    dop,
    table_sem,
    own_sem,
    send_x,
    recv_plane,
    recv_z,
    send_c,
    recv_c,
    ready,
):
    rx, tm = lax.axis_index("rx"), lax.axis_index("tm")
    count = planes * GROUP
    me = rx % GROUP
    base = rx - me
    below = (base + count - GROUP) % count
    above = (base + GROUP) % count

    def other(k):
        return (me // 2 + k // 2) % 2 * 2 + (me % 2 + k % 2) % 2

    def part_of_x(index, chunk):
        start = pl.multiple_of((index * CHUNKS + chunk) * CHUNK, CHUNK)
        return x_ref.at[:, pl.ds(start, CHUNK), :]

    def place(slot, chunk):
        return buf.at[slot, :, pl.ds(pl.multiple_of(chunk * CHUNK, CHUNK), CHUNK), :]

    own = pltpu.make_async_copy(
        x_ref.at[:, pl.ds(pl.multiple_of(me * SHARE * UNITS, UNITS), SHARE * UNITS), :],
        buf.at[me],
        own_sem,
    )

    def plane_copy(k, chunk):
        j = other(k)
        return pltpu.make_async_remote_copy(
            src_ref=part_of_x(j, chunk),
            dst_ref=place(me, chunk),
            send_sem=send_x.at[0],
            recv_sem=recv_plane.at[chunk],
            device_id=(base + j, tm),
            device_id_type=MESH,
        )

    def z_copy(k, chunk, src):
        j = other(k)
        return pltpu.make_async_remote_copy(
            src_ref=src,
            dst_ref=place(GROUP + j, chunk),
            send_sem=send_x.at[1],
            recv_sem=recv_z.at[chunk],
            device_id=((rx + count + (j // 2 * 2 - 1) * GROUP) % count, tm),
            device_id_type=MESH,
        )

    def received(ref, sem):
        return pltpu.make_async_remote_copy(
            src_ref=ref,
            dst_ref=ref,
            send_sem=send_c,
            recv_sem=sem,
            device_id=(rx, tm),
            device_id_type=MESH,
        )

    tables = [
        pltpu.make_async_copy(fwd_hbm, fwd, table_sem.at[0]),
        pltpu.make_async_copy(inv_hbm, inv, table_sem.at[1]),
        pltpu.make_async_copy(dop_hbm, dop, table_sem.at[2]),
    ]

    barrier = pltpu.get_barrier_semaphore()

    def greet(r, t):
        pl.semaphore_signal(barrier, 1, device_id=(r, t), device_id_type=MESH)

    greet(below + me, tm)
    greet(above + me, tm)
    for k in range(1, GROUP):
        greet(base + other(k), tm)
    for step in range(1, parts):
        greet(rx, (tm + step) % parts)
    for copy in tables:
        copy.start()
    own.start()
    pl.semaphore_wait(barrier, 2 + GROUP - 1 + parts - 1)

    for chunk in range(CHUNKS):
        for k in ((3, 2, 1) if chunk % 2 else (2, 3, 1)):
            plane_copy(k, chunk).start()
        z_copy(0, chunk, part_of_x(me, chunk)).start()

    for k in range(1, GROUP):
        pl.semaphore_signal(ready.at[0], 1, device_id=(base + other(k), tm), device_id_type=MESH)
    pl.semaphore_signal(ready.at[1], 1, device_id=(above + me, tm), device_id_type=MESH)
    tables[0].wait()
    pl.semaphore_wait(ready.at[1], 1)

    @pl.when(me < 2)
    def _():
        for k in range(GROUP):
            to = below + other(k)
            pl.semaphore_signal(ready.at[2], 1, device_id=(to, tm), device_id_type=MESH)

    def pieces(slot, seg, comp):
        rows = buf.at[slot, comp, pl.ds(pl.multiple_of(seg * UNITS, UNITS), UNITS), :]
        even = rows[pl.ds(0, BLOCKS, stride=2), :]
        odd = rows[pl.ds(1, BLOCKS, stride=2), :]
        return even, odd

    def window(slot, seg, comp):
        even, odd = pieces(slot, seg, comp)
        before = pltpu.roll(odd, 1, 0)
        after = pltpu.roll(even, BLOCKS - 1, 0)
        return jnp.concatenate([before, even, odd, after], axis=1)

    def window_spectra(slots, seg, side):
        rows = [window(slot, seg, comp) for comp in range(2) for slot in slots]
        mixed = product(jnp.concatenate(rows, axis=0), fwd[0], fwd[1])
        store_spectra(mixed, qs, side, slots[0] * BLOCKS)

    def block_spectra(slots, seg, side, target):
        rows = [
            jnp.concatenate(pieces(slot, seg, comp), axis=1) for comp in range(2) for slot in slots
        ]
        mixed = product(
            jnp.concatenate(rows, axis=0), fwd[0, : WINDOW // 2], fwd[1, : WINDOW // 2]
        )
        store_spectra(mixed, ps, side, target * BLOCKS)

    order = [(slot, off, far) for slot, partners in enumerate(PAIRS) for off, far in partners]
    order.sort(key=lambda entry: entry[0] >= GROUP or entry[2] >= GROUP - 1)
    inner = sum(slot < GROUP and far < GROUP - 1 for slot, _, far in order)

    def correlate(seg, first, last):
        def half_step(half, carry):
            def part(ref, slot, index):
                start = pl.multiple_of(index * (WINDOW // 2) + half * LANES, LANES)
                return ref[seg, slot * BLOCKS : (slot + 1) * BLOCKS, pl.ds(start, LANES)]

            for group in range(2):
                places = range(group * 8, group * 8 + 8)
                if not any(first <= place < last for place in places):
                    continue
                sums = []
                for place in places:
                    if not first <= place < last:
                        sums.append([None] * 4)
                        continue
                    slot, _, far = order[place]
                    q = [part(qs, slot, i) for i in range(4)]
                    p = [part(ps, far, i) for i in range(4)]
                    z = [
                        q[0] * p[0] + q[1] * p[1],
                        q[1] * p[0] - q[0] * p[1],
                        q[2] * p[2] + q[3] * p[3],
                        q[3] * p[2] - q[2] * p[3],
                    ]
                    z = [v[:8] + v[8:] for v in z]
                    sums.append([z[0] + z[2], z[3] - z[1], z[1] + z[3], z[0] - z[2]])
                for i in range(4):
                    row = pl.multiple_of(seg * 32 + i // 2 * 16 + group * 8, 8)
                    lane = pl.multiple_of(i % 2 * (WINDOW // 2) + half * LANES, LANES)
                    total = row_sums([v[i] for v in sums])
                    if places[0] < first:
                        total += srow[pl.ds(row, 8), pl.ds(lane, LANES)]
                    srow[pl.ds(row, 8), pl.ds(lane, LANES)] = total
            return carry

        lax.fori_loop(0, 2, half_step, 0)

    def arrived(slots, chunk, sem):
        received(place(slots, chunk), sem.at[chunk]).wait_recv()

    def seg_step(step, carry):
        @pl.when(step < SHARE)
        def _():
            for part in range(SPLIT):
                chunk = step * SPLIT + part
                arrived(slice(0, GROUP - 1), chunk, recv_plane)
                for k in (2, 3, 1):
                    z_copy(k, chunk, place(other(k), chunk)).start()

            @pl.when(step == 0)
            def _():
                own.wait()

            window_spectra(range(0, 4), step, step)
            block_spectra(range(0, 3), step, step, 0)
            correlate(step, 0, inner)

        @pl.when(step >= LAG_STEPS)
        def _():
            seg = step - LAG_STEPS
            for part in range(SPLIT):
                arrived(slice(GROUP, 2 * GROUP), seg * SPLIT + part, recv_z)
            window_spectra(range(4, 6), seg, seg)
            block_spectra(range(6, 8), seg, seg, 4)
            correlate(seg, inner, len(order))

        return carry

    lane = lax.broadcasted_iota(jnp.int32, (HALF_ROWS, LANES), 1)

    def tile_copy(k, step, half):
        j, to = other(k), (tm + step) % parts
        rows = pl.ds(half * HALF_ROWS, HALF_ROWS)
        return pltpu.make_async_remote_copy(
            src_ref=ct.at[j * parts + to, rows],
            dst_ref=fin.at[tm * GROUP + me, rows],
            send_sem=send_c,
            recv_sem=recv_c.at[0],
            device_id=(base + j, to),
            device_id_type=MESH,
        )

    def low_copy(i, step, half):
        to = (tm + step) % parts
        rows = pl.ds(half * HALF_ROWS, HALF_ROWS)
        return pltpu.make_async_remote_copy(
            src_ref=ct.at[(GROUP + i) * parts + to, rows],
            dst_ref=low.at[tm * GROUP + me, rows],
            send_sem=send_c,
            recv_sem=recv_c.at[1],
            device_id=(above + i, to),
            device_id_type=MESH,
        )

    def tiles(slots, half):
        first = half * SHARE * 16
        for slot in slots:
            for col in range(2):
                values = [
                    (off, corr[col, pl.ds(first + index, HALF_ROWS, stride=16), :])
                    for index, (at, off, _) in enumerate(order)
                    if at == slot
                ]
                for piece in range(4):
                    if col * 4 + piece >= parts:
                        continue
                    tile = jnp.zeros((HALF_ROWS, LANES), jnp.float32)
                    for off, value in values:
                        shift = LAG_DEV * (off - piece) % LANES
                        if shift:
                            value = pltpu.roll(value, shift, 1)
                        tile = jnp.where(lane // LAG_DEV == off, value, tile)
                    rows = slice(half * HALF_ROWS, (half + 1) * HALF_ROWS)
                    ct[slot * parts + col * 4 + piece, rows] = tile

    steps = sorted(range(parts), key=lambda step: -min(step % 4, -step % 4))

    def send_lags(half):
        rows = slice(half * SHARE * 16, (half + 1) * SHARE * 16)
        lags = product(srow[rows], inv[0], inv[1])
        corr[0, rows], corr[1, rows] = lags[:, :LANES], lags[:, LANES:]
        tiles((4, 5), half)
        for step in steps:
            for i in range(2):
                low_copy(i, step, half).start()
        tiles(range(4), half)
        for ks in ((3, 2), (1, 0)):
            for step in steps:
                for k in ks:
                    if k or step:
                        tile_copy(k, step, half).start()

    lax.fori_loop(0, SHARE // 2 + LAG_STEPS, seg_step, 0)
    tables[1].wait()
    pl.semaphore_wait(ready.at[0], GROUP - 1)
    pl.semaphore_wait(ready.at[2], 2)
    send_lags(0)
    lax.fori_loop(SHARE // 2 + LAG_STEPS, SHARE + LAG_STEPS, seg_step, 0)
    send_lags(1)

    fin[tm * GROUP + me] = ct[me * parts + tm]
    tables[2].wait()

    def sent(ref, sem):
        pltpu.make_async_remote_copy(
            src_ref=ref,
            dst_ref=ref,
            send_sem=sem,
            recv_sem=recv_c.at[0],
            device_id=(rx, tm),
            device_id_type=MESH,
        ).wait_send()

    sent(buf.at[: GROUP - 1], send_x.at[0])
    sent(buf.at[:GROUP], send_x.at[1])

    @pl.when(me < 2)
    def _():
        received(low, recv_c.at[1]).wait_recv()

    received(fin.at[: parts * GROUP - 1], recv_c.at[0]).wait_recv()

    rows = parts * GROUP * 2 * SHARE
    lanes = lax.broadcasted_iota(jnp.int32, (rows, LANES), 1)
    columns = jnp.where(
        lanes < 2 * LAG_DEV + LAG_DEV * me,
        fin[...].reshape(rows, LANES),
        low[...].reshape(rows, LANES),
    )
    result = product(columns.T, dop[0], dop[1])
    for off in range(OFFS):
        for col in range(4):
            out_ref[pl.ds(col // 2 * 8 + off * 2 + col % 2, LAG_DEV, stride=16), :] = result[
                off * LAG_DEV : (off + 1) * LAG_DEV, col * LANES : (col + 1) * LANES
            ]

    sent(ct.at[: 6 * parts - 1], send_c)


def per_device(planes, parts, signals):
    rows = signals.reshape(2, -1, LANES)
    dop_rows = parts * GROUP * 2 * SHARE
    dma, vmem = pltpu.SemaphoreType.DMA, pltpu.VMEM
    out = pl.pallas_call(
        functools.partial(kernel, planes, parts),
        out_shape=jax.ShapeDtypeStruct((LAG_DEV * 2 * OFFS * 2, LANES), jnp.float32),
        in_specs=[pl.BlockSpec(memory_space=pl.ANY)] * 4,
        out_specs=pl.BlockSpec(memory_space=pltpu.VMEM),
        scratch_shapes=[
            vmem((2 * GROUP, 2, SHARE * UNITS, LANES), jnp.float32),
            vmem((SHARE, 6 * BLOCKS, 2 * WINDOW), jnp.float32),
            vmem((SHARE, 6 * BLOCKS, 2 * WINDOW), jnp.float32),
            vmem((SHARE * 32, WINDOW), jnp.float32),
            vmem((2, SHARE * 32, LANES), jnp.float32),
            vmem((6 * parts, 8, LANES), jnp.float32),
            vmem((parts * GROUP, 8, LANES), jnp.float32),
            vmem((parts * GROUP, 8, LANES), jnp.float32),
            vmem((2, WINDOW, WINDOW), jnp.bfloat16),
            vmem((2, WINDOW, LAGS), jnp.bfloat16),
            vmem((2, dop_rows, 2 * DOPK), jnp.bfloat16),
            dma((3,)),
            dma,
            dma((2,)),
            dma((CHUNKS,)),
            dma((CHUNKS,)),
            dma,
            dma((2,)),
            pltpu.SemaphoreType.REGULAR((3,)),
        ],
        compiler_params=pltpu.CompilerParams(
            collective_id=0, has_side_effects=True, vmem_limit_bytes=VMEM_LIMIT
        ),
        name="ambiguity",
    )(
        rows,
        jnp.asarray(forward_table()),
        jnp.asarray(inverse_table()),
        jnp.asarray(doppler_table(parts)),
    )
    scale = 1.0 / math.sqrt(2.0 * SEG_LEN * parts * GROUP * SHARE)
    return out.reshape(LAG_DEV, 2, 1, OFFS, 1, DOPK) * jnp.float32(scale)


def solution(mesh):
    planes, parts = mesh.shape["rx"] // GROUP, mesh.shape["tm"]
    return jax.shard_map(
        functools.partial(per_device, planes, parts),
        mesh=mesh,
        in_specs=(P(None, "rx", "tm"),),
        out_specs=P("tm", None, "rx", None, None, None),
        check_vma=False,
    )
```

```python
import functools
import math

import jax
import jax.numpy as jnp
import ml_dtypes
import numpy as np
from jax import lax
from jax.experimental import pallas as pl
from jax.experimental.pallas import tpu as pltpu
from jax.sharding import PartitionSpec as P

SEG_LEN = 4096
LAGS = 256
DOPLEN = 512
DOPK = 256
OFFS = 4
WINDOW = 512
LANES = 128
GROUP = 4
SHARE = 4
UNITS = SEG_LEN // LANES
BLOCKS = SEG_LEN // 256
LAG_DEV = 32
HALF_ROWS = SHARE
SPLIT = 2
CHUNKS = SHARE * SPLIT
LAG_STEPS = 3
CHUNK = UNITS // SPLIT
VMEM_LIMIT = 67043328 - 10800 * 1024

MESH = pl.DeviceIdType.MESH

PAIRS = (
    ((0, 5), (1, 4)),
    ((0, 0), (1, 5), (2, 4)),
    ((0, 1), (1, 0), (2, 5), (3, 4)),
    ((0, 2), (1, 1), (2, 0), (3, 5)),
    ((2, 1), (3, 0)),
    ((3, 1),),
)


def split_table(table):
    table = table.astype(np.float32)
    high = table.astype(ml_dtypes.bfloat16)
    low = (table - high.astype(np.float32)).astype(ml_dtypes.bfloat16)
    return np.stack([high, low])


def forward_table():
    sample = np.arange(WINDOW)[:, None]
    freq = np.arange(WINDOW // 2)[None, :] + 0.5
    angle = 2.0 * np.pi / WINDOW * sample * freq
    return split_table(np.concatenate([np.cos(angle), np.sin(angle)], axis=1))


def inverse_table():
    lag = np.arange(LAGS)[None, :]
    freq = np.arange(WINDOW // 2)[:, None] + 0.5
    angle = 2.0 * np.pi / WINDOW * lag * freq
    return split_table(np.concatenate([np.cos(angle), np.sin(angle)], axis=0) / WINDOW)


def doppler_table(parts):
    seg = np.arange(parts * GROUP * SHARE).reshape(parts, GROUP, SHARE, 1)
    freq = np.arange(DOPK) - DOPK // 2
    angle = 2.0 * np.pi / DOPLEN * (seg * freq % DOPLEN)
    cos, sin = np.cos(angle), -np.sin(angle)
    real_rows = np.concatenate([cos, sin], axis=-1)
    imag_rows = np.concatenate([-sin, cos], axis=-1)
    table = np.stack([real_rows, imag_rows], axis=3)
    return split_table(table.reshape(parts * GROUP * 2 * SHARE, 2 * DOPK))


def halves(value):
    high = value.astype(jnp.bfloat16)
    low = (value - high.astype(jnp.float32)).astype(jnp.bfloat16)
    return high, low


def product(value, high_table, low_table):
    rows = value.shape[0]
    high, low = halves(value)
    both = jnp.dot(
        jnp.concatenate([high, low], axis=0), high_table, preferred_element_type=jnp.float32
    )
    small = jnp.dot(high, low_table, preferred_element_type=jnp.float32)
    return both[:rows] + (both[rows:] + small)


def store_spectra(mixed, ref, side, start):
    rows, half = mixed.shape[0] // 2, mixed.shape[1] // 2
    a_cos, a_sin = mixed[:rows, :half], mixed[:rows, half:]
    b_cos, b_sin = mixed[rows:, :half], mixed[rows:, half:]
    parts = (a_cos + b_sin, b_cos - a_sin, a_cos - b_sin, b_cos + a_sin)
    for index, part in enumerate(parts):
        ref[side, start : start + rows, index * half : (index + 1) * half] = part


def row_sums(values):
    index = lax.broadcasted_iota(jnp.int32, (8, LANES), 0)
    zero = jnp.zeros((8, LANES), jnp.float32)
    step = 1
    while len(values) > 1:
        first = index // step % 2 == 0
        pairs = list(zip(values[0::2], values[1::2]))
        values = []
        for a, b in pairs:
            if a is None and b is None:
                values.append(None)
                continue
            a, b = zero if a is None else a, zero if b is None else b
            values.append(jnp.where(first, a, b) + pltpu.roll(jnp.where(first, b, a), step, 0))
        step *= 2
    return values[0]


def kernel(
    planes,
    parts,
    x_ref,
    fwd_hbm,
    inv_hbm,
    dop_hbm,
    out_ref,
    buf,
    qs,
    ps,
    srow,
    corr,
    ct,
    fin,
    low,
    fwd,
    inv,
    dop,
    table_sem,
    own_sem,
    send_x,
    recv_plane,
    recv_z,
    send_c,
    recv_c,
    ready,
):
    rx, tm = lax.axis_index("rx"), lax.axis_index("tm")
    count = planes * GROUP
    me = rx % GROUP
    base = rx - me
    below = (base + count - GROUP) % count
    above = (base + GROUP) % count

    def other(k):
        return (me // 2 + k // 2) % 2 * 2 + (me % 2 + k % 2) % 2

    def part_of_x(index, chunk):
        start = pl.multiple_of((index * CHUNKS + chunk) * CHUNK, CHUNK)
        return x_ref.at[:, pl.ds(start, CHUNK), :]

    def place(slot, chunk):
        return buf.at[slot, :, pl.ds(pl.multiple_of(chunk * CHUNK, CHUNK), CHUNK), :]

    own = pltpu.make_async_copy(
        x_ref.at[:, pl.ds(pl.multiple_of(me * SHARE * UNITS, UNITS), SHARE * UNITS), :],
        buf.at[me],
        own_sem,
    )

    def plane_copy(k, chunk):
        j = other(k)
        return pltpu.make_async_remote_copy(
            src_ref=part_of_x(j, chunk),
            dst_ref=place(me, chunk),
            send_sem=send_x.at[0],
            recv_sem=recv_plane.at[chunk],
            device_id=(base + j, tm),
            device_id_type=MESH,
        )

    def z_copy(k, chunk, src):
        j = other(k)
        return pltpu.make_async_remote_copy(
            src_ref=src,
            dst_ref=place(GROUP + j, chunk),
            send_sem=send_x.at[1],
            recv_sem=recv_z.at[chunk],
            device_id=((rx + count + (j // 2 * 2 - 1) * GROUP) % count, tm),
            device_id_type=MESH,
        )

    def received(ref, sem):
        return pltpu.make_async_remote_copy(
            src_ref=ref,
            dst_ref=ref,
            send_sem=send_c,
            recv_sem=sem,
            device_id=(rx, tm),
            device_id_type=MESH,
        )

    tables = [
        pltpu.make_async_copy(fwd_hbm, fwd, table_sem.at[0]),
        pltpu.make_async_copy(inv_hbm, inv, table_sem.at[1]),
        pltpu.make_async_copy(dop_hbm, dop, table_sem.at[2]),
    ]

    barrier = pltpu.get_barrier_semaphore()

    def greet(r, t):
        pl.semaphore_signal(barrier, 1, device_id=(r, t), device_id_type=MESH)

    greet(below + me, tm)
    greet(above + me, tm)
    for k in range(1, GROUP):
        greet(base + other(k), tm)
    for step in range(1, parts):
        greet(rx, (tm + step) % parts)
    for copy in tables:
        copy.start()
    own.start()
    pl.semaphore_wait(barrier, 2 + GROUP - 1 + parts - 1)

    for chunk in range(CHUNKS):
        for k in ((3, 2, 1) if chunk % 2 else (2, 3, 1)):
            plane_copy(k, chunk).start()
        z_copy(0, chunk, part_of_x(me, chunk)).start()

    for k in range(1, GROUP):
        pl.semaphore_signal(ready.at[0], 1, device_id=(base + other(k), tm), device_id_type=MESH)
    pl.semaphore_signal(ready.at[1], 1, device_id=(above + me, tm), device_id_type=MESH)
    tables[0].wait()
    pl.semaphore_wait(ready.at[1], 1)

    @pl.when(me < 2)
    def _():
        for k in range(GROUP):
            to = below + other(k)
            pl.semaphore_signal(ready.at[2], 1, device_id=(to, tm), device_id_type=MESH)

    def pieces(slot, seg, comp):
        rows = buf.at[slot, comp, pl.ds(pl.multiple_of(seg * UNITS, UNITS), UNITS), :]
        even = rows[pl.ds(0, BLOCKS, stride=2), :]
        odd = rows[pl.ds(1, BLOCKS, stride=2), :]
        return even, odd

    def window(slot, seg, comp):
        even, odd = pieces(slot, seg, comp)
        before = pltpu.roll(odd, 1, 0)
        after = pltpu.roll(even, BLOCKS - 1, 0)
        return jnp.concatenate([before, even, odd, after], axis=1)

    def window_spectra(slots, seg, side):
        rows = [window(slot, seg, comp) for comp in range(2) for slot in slots]
        mixed = product(jnp.concatenate(rows, axis=0), fwd[0], fwd[1])
        store_spectra(mixed, qs, side, slots[0] * BLOCKS)

    def block_spectra(slots, seg, side, target):
        rows = [
            jnp.concatenate(pieces(slot, seg, comp), axis=1) for comp in range(2) for slot in slots
        ]
        mixed = product(
            jnp.concatenate(rows, axis=0), fwd[0, : WINDOW // 2], fwd[1, : WINDOW // 2]
        )
        store_spectra(mixed, ps, side, target * BLOCKS)

    order = [(slot, off, far) for slot, partners in enumerate(PAIRS) for off, far in partners]
    order.sort(key=lambda entry: entry[0] >= GROUP or entry[2] >= GROUP - 1)
    inner = sum(slot < GROUP and far < GROUP - 1 for slot, _, far in order)

    def correlate(seg, first, last):
        def half_step(half, carry):
            def part(ref, slot, index):
                start = pl.multiple_of(index * (WINDOW // 2) + half * LANES, LANES)
                return ref[seg, slot * BLOCKS : (slot + 1) * BLOCKS, pl.ds(start, LANES)]

            for group in range(2):
                places = range(group * 8, group * 8 + 8)
                if not any(first <= place < last for place in places):
                    continue
                sums = []
                for place in places:
                    if not first <= place < last:
                        sums.append([None] * 4)
                        continue
                    slot, _, far = order[place]
                    q = [part(qs, slot, i) for i in range(4)]
                    p = [part(ps, far, i) for i in range(4)]
                    z = [
                        q[0] * p[0] + q[1] * p[1],
                        q[1] * p[0] - q[0] * p[1],
                        q[2] * p[2] + q[3] * p[3],
                        q[3] * p[2] - q[2] * p[3],
                    ]
                    z = [v[:8] + v[8:] for v in z]
                    sums.append([z[0] + z[2], z[3] - z[1], z[1] + z[3], z[0] - z[2]])
                for i in range(4):
                    row = pl.multiple_of(seg * 32 + i // 2 * 16 + group * 8, 8)
                    lane = pl.multiple_of(i % 2 * (WINDOW // 2) + half * LANES, LANES)
                    total = row_sums([v[i] for v in sums])
                    if places[0] < first:
                        total += srow[pl.ds(row, 8), pl.ds(lane, LANES)]
                    srow[pl.ds(row, 8), pl.ds(lane, LANES)] = total
            return carry

        lax.fori_loop(0, 2, half_step, 0)

    def arrived(slots, chunk, sem):
        received(place(slots, chunk), sem.at[chunk]).wait_recv()

    def seg_step(step, carry):
        @pl.when(step < SHARE)
        def _():
            for part in range(SPLIT):
                chunk = step * SPLIT + part
                arrived(slice(0, GROUP - 1), chunk, recv_plane)
                for k in ((3, 2, 1) if part else (2, 3, 1)):
                    z_copy(k, chunk, place(other(k), chunk)).start()

            @pl.when(step == 0)
            def _():
                own.wait()

            window_spectra(range(0, 4), step, step)
            block_spectra(range(0, 3), step, step, 0)
            correlate(step, 0, inner)

        @pl.when(step >= LAG_STEPS)
        def _():
            seg = step - LAG_STEPS
            for part in range(SPLIT):
                arrived(slice(GROUP, 2 * GROUP), seg * SPLIT + part, recv_z)
            window_spectra(range(4, 6), seg, seg)
            block_spectra(range(6, 8), seg, seg, 4)
            correlate(seg, inner, len(order))

        return carry

    lane = lax.broadcasted_iota(jnp.int32, (HALF_ROWS, LANES), 1)

    def tile_copy(k, step, half):
        j, to = other(k), (tm + step) % parts
        rows = pl.ds(half * HALF_ROWS, HALF_ROWS)
        return pltpu.make_async_remote_copy(
            src_ref=ct.at[j * parts + to, rows],
            dst_ref=fin.at[tm * GROUP + me, rows],
            send_sem=send_c,
            recv_sem=recv_c.at[0],
            device_id=(base + j, to),
            device_id_type=MESH,
        )

    def low_copy(i, step, half):
        to = (tm + step) % parts
        rows = pl.ds(half * HALF_ROWS, HALF_ROWS)
        return pltpu.make_async_remote_copy(
            src_ref=ct.at[(GROUP + i) * parts + to, rows],
            dst_ref=low.at[tm * GROUP + me, rows],
            send_sem=send_c,
            recv_sem=recv_c.at[1],
            device_id=(above + i, to),
            device_id_type=MESH,
        )

    def tiles(slots, half):
        first = half * SHARE * 16
        for slot in slots:
            for col in range(2):
                values = [
                    (off, corr[col, pl.ds(first + index, HALF_ROWS, stride=16), :])
                    for index, (at, off, _) in enumerate(order)
                    if at == slot
                ]
                for piece in range(4):
                    if col * 4 + piece >= parts:
                        continue
                    tile = jnp.zeros((HALF_ROWS, LANES), jnp.float32)
                    for off, value in values:
                        shift = LAG_DEV * (off - piece) % LANES
                        if shift:
                            value = pltpu.roll(value, shift, 1)
                        tile = jnp.where(lane // LAG_DEV == off, value, tile)
                    rows = slice(half * HALF_ROWS, (half + 1) * HALF_ROWS)
                    ct[slot * parts + col * 4 + piece, rows] = tile

    steps = sorted(range(parts), key=lambda step: -min(step % 4, -step % 4))

    def send_lags(half):
        rows = slice(half * SHARE * 16, (half + 1) * SHARE * 16)
        lags = product(srow[rows], inv[0], inv[1])
        corr[0, rows], corr[1, rows] = lags[:, :LANES], lags[:, LANES:]
        tiles((4, 5), half)
        for step in steps:
            for i in range(2):
                low_copy(i, step, half).start()
        tiles(range(4), half)
        for ks in ((3, 2), (1, 0)):
            for step in steps:
                for k in ks:
                    if k or step:
                        tile_copy(k, step, half).start()

    lax.fori_loop(0, SHARE // 2 + LAG_STEPS, seg_step, 0)
    tables[1].wait()
    pl.semaphore_wait(ready.at[0], GROUP - 1)
    pl.semaphore_wait(ready.at[2], 2)
    send_lags(0)
    lax.fori_loop(SHARE // 2 + LAG_STEPS, SHARE + LAG_STEPS, seg_step, 0)
    send_lags(1)

    fin[tm * GROUP + me] = ct[me * parts + tm]
    tables[2].wait()

    def sent(ref, sem):
        pltpu.make_async_remote_copy(
            src_ref=ref,
            dst_ref=ref,
            send_sem=sem,
            recv_sem=recv_c.at[0],
            device_id=(rx, tm),
            device_id_type=MESH,
        ).wait_send()

    sent(buf.at[: GROUP - 1], send_x.at[0])
    sent(buf.at[:GROUP], send_x.at[1])

    @pl.when(me < 2)
    def _():
        received(low, recv_c.at[1]).wait_recv()

    received(fin.at[: parts * GROUP - 1], recv_c.at[0]).wait_recv()

    rows = parts * GROUP * 2 * SHARE
    lanes = lax.broadcasted_iota(jnp.int32, (rows, LANES), 1)
    columns = jnp.where(
        lanes < 2 * LAG_DEV + LAG_DEV * me,
        fin[...].reshape(rows, LANES),
        low[...].reshape(rows, LANES),
    )
    result = product(columns.T, dop[0], dop[1])
    for off in range(OFFS):
        for col in range(4):
            out_ref[pl.ds(col // 2 * 8 + off * 2 + col % 2, LAG_DEV, stride=16), :] = result[
                off * LAG_DEV : (off + 1) * LAG_DEV, col * LANES : (col + 1) * LANES
            ]

    sent(ct.at[: 6 * parts - 1], send_c)


def per_device(planes, parts, signals):
    rows = signals.reshape(2, -1, LANES)
    dop_rows = parts * GROUP * 2 * SHARE
    dma, vmem = pltpu.SemaphoreType.DMA, pltpu.VMEM
    out = pl.pallas_call(
        functools.partial(kernel, planes, parts),
        out_shape=jax.ShapeDtypeStruct((LAG_DEV * 2 * OFFS * 2, LANES), jnp.float32),
        in_specs=[pl.BlockSpec(memory_space=pl.ANY)] * 4,
        out_specs=pl.BlockSpec(memory_space=pltpu.VMEM),
        scratch_shapes=[
            vmem((2 * GROUP, 2, SHARE * UNITS, LANES), jnp.float32),
            vmem((SHARE, 6 * BLOCKS, 2 * WINDOW), jnp.float32),
            vmem((SHARE, 6 * BLOCKS, 2 * WINDOW), jnp.float32),
            vmem((SHARE * 32, WINDOW), jnp.float32),
            vmem((2, SHARE * 32, LANES), jnp.float32),
            vmem((6 * parts, 8, LANES), jnp.float32),
            vmem((parts * GROUP, 8, LANES), jnp.float32),
            vmem((parts * GROUP, 8, LANES), jnp.float32),
            vmem((2, WINDOW, WINDOW), jnp.bfloat16),
            vmem((2, WINDOW, LAGS), jnp.bfloat16),
            vmem((2, dop_rows, 2 * DOPK), jnp.bfloat16),
            dma((3,)),
            dma,
            dma((2,)),
            dma((CHUNKS,)),
            dma((CHUNKS,)),
            dma,
            dma((2,)),
            pltpu.SemaphoreType.REGULAR((3,)),
        ],
        compiler_params=pltpu.CompilerParams(
            collective_id=0, has_side_effects=True, vmem_limit_bytes=VMEM_LIMIT
        ),
        name="ambiguity",
    )(
        rows,
        jnp.asarray(forward_table()),
        jnp.asarray(inverse_table()),
        jnp.asarray(doppler_table(parts)),
    )
    scale = 1.0 / math.sqrt(2.0 * SEG_LEN * parts * GROUP * SHARE)
    return out.reshape(LAG_DEV, 2, 1, OFFS, 1, DOPK) * jnp.float32(scale)


def solution(mesh):
    planes, parts = mesh.shape["rx"] // GROUP, mesh.shape["tm"]
    return jax.shard_map(
        functools.partial(per_device, planes, parts),
        mesh=mesh,
        in_specs=(P(None, "rx", "tm"),),
        out_specs=P("tm", None, "rx", None, None, None),
        check_vma=False,
    )
```
